128 devices in a mesh: band: 8 (over z_hi, x), slab: 16 (over z_lo, y, core).
Axes of the slice: x: 4, y: 4, z: 4 (z_hi: 2, z_lo: 2; z = z_hi * 2 + z_lo), core: 2. Of those that a mesh axis runs over, the one named last changes fastest.
Arguments:
- orbitals: bfloat16 [32, 256, 256, 256], P('band', 'slab'), may hold values from -6 to 6
- occupation: float32 [32], P('band'), may hold values from 0.2 to 2
Outputs:
- density: float32 [256, 256, 256], P('slab', 'band')
- hartree: float32 [256, 256, 256], P('slab', 'band')
The draws below stay inside these ranges and needn't reach their ends.
All inputs are finite; a program needn't handle non-finite values.
Results may differ from the reference program's by a relative error of at most 0.0019.
Values sent between devices are 32-bit elements; how exact they have to be, the bound alone decides.
No kernel may reach another device: no remote copies, remote signals or barrier semaphores. Data moves between devices by JAX's collectives and lax.ppermute only.
A program may use at most 128 MiB of HBM per device.

```python
import math
import jax
import jax.numpy as jnp
from jax import lax

GRID = 256
BANDS = 32


def draw_orbitals(key, part):
    scale_key = jax.random.fold_in(key, 11)
    entry_key = jax.random.fold_in(key, 29)
    scales = jnp.exp(jax.random.uniform(scale_key, (BANDS,), jnp.float32, math.log(0.6), math.log(1.6)))

    def one_band(band_index):
        band_key = jax.random.fold_in(entry_key, band_index)
        values = jax.random.normal(band_key, (GRID, GRID, GRID), jnp.float32)
        return jnp.clip(values * scales[band_index], -6.0, 6.0).astype(jnp.bfloat16)
    return lax.map(one_band, jnp.arange(BANDS, dtype=jnp.int32))


def levels(stream_key, shape, cuts, smallest, high):
    def one(position, blocks):
        heights = jax.random.uniform(jax.random.fold_in(jax.random.fold_in(stream_key, 6), position), (blocks,), jnp.float32, smallest / len(cuts), high / len(cuts))
        return jnp.repeat(jnp.exp(heights), shape[position] // blocks).reshape((-1,) + (1,) * (len(shape) - position - 1))

    level = one(*cuts[0])
    for cut in cuts[1:]:
        level = level * one(*cut)
    return level


def setup_inputs(seed: int = 0) -> dict:
    key_of = jax.random.split(jax.random.key(seed), 3)
    orbitals = draw_orbitals(jax.random.fold_in(key_of[2], 71), 0)
    occupation = jnp.clip(0.2 + 1.8 * jax.random.uniform(key_of[1], (BANDS,), jnp.float32) ** levels(key_of[1], (BANDS,), ((0, 8),), -0.2, 0.2), 0.2, 2.0)
    return {"orbitals": orbitals, "occupation": occupation}


spacing = 0.08


def signed_freq(count):
    indices = jnp.arange(count, dtype=jnp.int32)
    return jnp.where(indices < count // 2, indices, indices - count).astype(jnp.float32)


def green_table(freq_z, freq_x, freq_y, count):
    scale = (2.0 * math.pi / (count * spacing)) ** 2
    wave_sq = scale * (freq_z * freq_z + freq_x * freq_x + freq_y * freq_y)
    anchor = wave_sq == 0.0
    return jnp.where(anchor, 0.0, 4.0 * math.pi / (wave_sq + anchor.astype(jnp.float32)))


def reference(orbitals, occupation):
    def accumulate(total, pieces):
        values = pieces[0].astype(jnp.float32)
        return total + pieces[1] * values * values, None

    start = jnp.zeros(orbitals.shape[1:], jnp.float32)
    density, unused = lax.scan(accumulate, start, (orbitals, occupation))
    spectrum = jnp.fft.fftn(density)
    freq = signed_freq(GRID)
    green = green_table(freq[:, None, None], freq[None, :, None], freq[None, None, :], GRID)
    hartree = jnp.real(jnp.fft.ifftn(spectrum * green)).astype(jnp.float32)
    return density, hartree
```

```python
import math

import jax
import jax.numpy as jnp
import numpy as np
from jax import lax
from jax.experimental import pallas as pl
from jax.experimental.pallas import tpu as pltpu
from jax.sharding import PartitionSpec as P

spacing = 0.08
axes = ("band", "slab")


def circle_tables(count):
    quarter = count // 4
    eighth = np.sin(2.0 * np.pi * np.arange(quarter + 1) / count)
    eighth[quarter] = 1.0
    first = np.concatenate([eighth[:quarter], eighth[:0:-1]])
    sine = np.concatenate([first, -first])
    cosine = np.roll(sine, -quarter)
    return cosine, sine


def split_table(table):
    high = table.astype(jnp.bfloat16)
    low = (table - high.astype(np.float64)).astype(jnp.bfloat16)
    return high, low


def dft_tables(count):
    cosine, sine = circle_tables(count)
    phases = np.arange(count)[:, None] * np.arange(count)[None, :] % count
    return cosine[phases], sine[phases]


def line_tables(count):
    cosine, sine = dft_tables(count)
    half = count // 2
    real_rows = cosine[:half].copy()
    imag_rows = -sine[:half]
    imag_rows[0] = cosine[half]
    return real_rows, imag_rows


def split(values):
    high = values.astype(jnp.bfloat16)
    low = (values - high.astype(jnp.float32)).astype(jnp.bfloat16)
    return high, low


def dot3(left, right, dims):
    def one(a, b):
        return lax.dot_general(a, b, (dims, ((), ())), preferred_element_type=jnp.float32)

    return one(left[0], right[0]) + (one(left[1], right[0]) + one(left[0], right[1]))


plain = ((1,), (0,))
rows_rows = ((1,), (1,))
cols_cols = ((0,), (0,))


def swap_blocks(parts):
    lane = lax.broadcasted_iota(jnp.int32, parts[0].shape, len(parts[0].shape) - 1)
    axis = len(parts[0].shape) - 1
    even = (lane // 32) % 2 == 0
    low = lane < 64
    pairs = []
    for first, second in ((parts[0], parts[1]), (parts[2], parts[3])):
        pairs.append(
            (
                jnp.where(even, first, pltpu.roll(second, 32, axis)),
                jnp.where(even, pltpu.roll(first, 96, axis), second),
            )
        )
    (a0, a1), (b0, b1) = pairs
    return (
        jnp.where(low, a0, pltpu.roll(b0, 64, axis)),
        jnp.where(low, a1, pltpu.roll(b1, 64, axis)),
        jnp.where(low, pltpu.roll(a0, 64, axis), b0),
        jnp.where(low, pltpu.roll(a1, 64, axis), b1),
    )


def forward_kernel(upper_ref, lower_ref, rh_ref, rl_ref, ih_ref, il_ref, out_ref):
    rows = jnp.concatenate([half[zq] for zq in range(8) for half in (upper_ref, lower_ref)], axis=0)
    mean = jnp.sum(rows) * (1.0 / rows.size)
    operand = split(rows - mean)
    real = dot3((rh_ref[...], rl_ref[...]), operand, rows_rows)
    zero = lax.broadcasted_iota(jnp.int32, real.shape, 0) == 0
    real = real + jnp.where(zero, mean * rows.shape[1], 0.0)
    imag = dot3((ih_ref[...], il_ref[...]), operand, rows_rows)
    low = lax.broadcasted_iota(jnp.int32, (128, 128), 1) < 64
    for pair in range(4):
        a = real[:, pair * 128 : (pair + 1) * 128]
        b = imag[:, pair * 128 : (pair + 1) * 128]
        out_ref[:, 2 * pair, :] = jnp.where(low, a, pltpu.roll(b, 64, 1))
        out_ref[:, 2 * pair + 1, :] = jnp.where(low, pltpu.roll(a, 64, 1), b)


def plane_kernel(freq_ref, message_ref, ch_ref, cl_ref, sh_ref, sl_ref, out_ref):
    count = 256
    cosine = (ch_ref[...], cl_ref[...])
    sine = (sh_ref[...], sl_ref[...])
    columns = [[], []]
    for group in range(2):
        parts = [
            message_ref[(group * 4 + member) * 16 : (group * 4 + member + 1) * 16]
            for member in range(4)
        ]
        blocks = swap_blocks(parts)
        for part in range(2):
            whole = jnp.stack([blocks[part * 2], blocks[part * 2 + 1]], axis=1)
            columns[part].append(whole.reshape(count, 128))
    planes = [jnp.concatenate(columns[part], axis=1) for part in range(2)]
    means = [jnp.sum(part) * (1.0 / count**2) for part in planes]
    operand = split(jnp.concatenate([part - mean for part, mean in zip(planes, means)], axis=0))
    by_cos = dot3(operand, cosine, plain)
    by_sin = dot3(operand, sine, plain)
    real = by_cos[:count] + by_sin[count:]
    imag = by_cos[count:] - by_sin[:count]
    operand = split(jnp.concatenate([real, imag], axis=1))
    by_cos = dot3(cosine, operand, plain)
    by_sin = dot3(sine, operand, plain)
    real = by_cos[:, :count] + by_sin[:, count:]
    imag = by_cos[:, count:] - by_sin[:, :count]

    def signed(axis):
        index = lax.broadcasted_iota(jnp.int32, (count, count), axis)
        return jnp.where(index < count // 2, index, index - count).astype(jnp.float32)

    freq_z = signed(0)
    freq_x = signed(1)
    plane_sq = freq_z * freq_z + freq_x * freq_x
    zero = plane_sq == 0.0
    real = real + jnp.where(zero, means[0] * count**2, 0.0)
    imag = imag + jnp.where(zero, means[1] * count**2, 0.0)
    scale = (2.0 * math.pi / (count * spacing)) ** 2

    def green(freq_y):
        wave_sq = scale * (plane_sq + freq_y * freq_y)
        anchor = wave_sq == 0.0
        return jnp.where(
            anchor, 0.0, (4.0 * math.pi / count**3) / (wave_sq + anchor.astype(jnp.float32))
        )

    green_a = green(freq_ref[0])
    green_b = green(freq_ref[1])
    operand = split(
        jnp.concatenate([real * green_a, imag * green_a, real * green_b, imag * green_b], axis=1)
    )
    by_cos = dot3(cosine, operand, plain)
    by_sin = dot3(sine, operand, plain)
    real_a = by_cos[:, :count] - by_sin[:, count : 2 * count]
    imag_a = by_cos[:, count : 2 * count] + by_sin[:, :count]
    real_b = by_cos[:, 2 * count : 3 * count] - by_sin[:, 3 * count :]
    imag_b = by_cos[:, 3 * count :] + by_sin[:, 2 * count : 3 * count]
    result = dot3(split(jnp.concatenate([real_a, imag_b], axis=0)), cosine, plain) + dot3(
        split(jnp.concatenate([-imag_a, real_b], axis=0)), sine, plain
    )
    for group in range(2):
        blocks = []
        for part in range(2):
            whole = result[part * count : (part + 1) * count, group * 128 : (group + 1) * 128]
            whole = whole.reshape(16, 2, 8, 128)
            blocks += [whole[:, 0], whole[:, 1]]
        for member, values in enumerate(swap_blocks(blocks)):
            out_ref[(group * 4 + member) * 16 : (group * 4 + member + 1) * 16] = values


def inverse_kernel(message_ref, rh_ref, rl_ref, ih_ref, il_ref, out_ref):
    real_table = (rh_ref[...], rl_ref[...])
    imag_table = (ih_ref[...], il_ref[...])
    for zq in range(8):
        rows = message_ref[:, zq, :].T
        real = dot3(split(rows[:64]), real_table, plain)
        imag = dot3(split(rows[64:]), imag_table, plain)
        lines = real + imag
        out_ref[zq] = lines[:32]
        out_ref[zq + 8] = lines[32:]


def density_kernel(pieces, start_ref, occupation_ref, orbitals_ref, *refs):
    outs, (buffer, sems) = refs[:-2], refs[-2:]
    flat = [piece for group in pieces for piece in group]
    copies = []
    for slot, (half, dx, dz) in enumerate(flat):
        block = (start_ref[0] + dz) % 2 * 4 + (start_ref[1] + dx) % 4
        source = orbitals_ref.at[:, pl.ds(half * 8, 8), pl.ds(block * 32, 32), :]
        copies.append(pltpu.make_async_copy(source, buffer.at[slot], sems.at[slot]))
    for copy in copies:
        copy.start()
    weights = [occupation_ref[band] for band in range(4)]
    slot = 0
    for out, group in zip(outs, pieces):
        for place in range(len(group)):
            copies[slot].wait()
            total = None
            for band in range(4):
                values = buffer[slot, band].astype(jnp.float32)
                term = values * values * weights[band]
                total = term if total is None else total + term
            if len(group) == 1:
                out[...] = total
            else:
                out[place] = total
            slot += 1


def partial_densities(orbitals, occupation, start, pieces, name):
    shapes = [
        pltpu.VMEM((8, 32, 256) if len(g) == 1 else (len(g), 8, 32, 256), jnp.float32)
        for g in pieces
    ]
    count = sum(len(g) for g in pieces)
    return pl.pallas_call(
        lambda *refs: density_kernel(pieces, *refs),
        out_shape=shapes,
        in_specs=[
            pl.BlockSpec(memory_space=pltpu.SMEM),
            pl.BlockSpec(memory_space=pltpu.SMEM),
            pl.BlockSpec(memory_space=pl.ANY),
        ],
        out_specs=[pl.BlockSpec(memory_space=pltpu.VMEM)] * len(shapes),
        scratch_shapes=[
            pltpu.VMEM((count, 4, 8, 32, 256), jnp.bfloat16),
            pltpu.SemaphoreType.DMA((count,)),
        ],
        name=name,
    )(start, occupation, orbitals)


def vmem_call(kernel, out_shape, name, operands, scalars=0):
    placed = [pltpu.with_memory_space_constraint(value, pltpu.VMEM) for value in operands[scalars:]]
    vmem = pl.BlockSpec(memory_space=pltpu.VMEM)
    return pl.pallas_call(
        kernel,
        out_shape=out_shape,
        in_specs=[pl.BlockSpec(memory_space=pltpu.SMEM)] * scalars + [vmem] * len(placed),
        out_specs=jax.tree.map(lambda shape: vmem, out_shape),
        name=name,
    )(*operands[:scalars], *placed)


def per_device(orbitals, occupation):
    count = orbitals.shape[2]
    half = count // 2
    upper, lower = band_sum(orbitals, occupation)

    forward_real, forward_imag = line_tables(count)
    tables = [*split_table(forward_real), *split_table(forward_imag)]
    block = jax.ShapeDtypeStruct((16, 32, count), jnp.float32)
    exchanged = pltpu.VMEM((half, 8, 128), jnp.float32)
    message = vmem_call(forward_kernel, exchanged, "forward_lines", (upper, lower, *tables))
    density = jnp.concatenate([upper, lower], axis=0)
    message = lax.all_to_all(message, axes, 0, 0, tiled=True)

    rank = lax.axis_index("band") * lax.axis_size("slab") + lax.axis_index("slab")
    freq = jnp.stack([rank, jnp.where(rank == 0, half, rank)]).astype(jnp.float32)
    cosine, sine = dft_tables(count)
    tables = [*split_table(cosine), *split_table(sine)]
    message = vmem_call(plane_kernel, exchanged, "plane_solve", (freq, message, *tables), 1)
    message = lax.all_to_all(message, axes, 0, 0, tiled=True)

    weight = np.full((half, 1), 2.0)
    weight[0] = 1.0
    tables = [*split_table(forward_real * weight), *split_table(forward_imag * weight)]
    potential = vmem_call(inverse_kernel, block, "inverse_lines", (message, *tables))
    return density, potential


def ring(dx, dz):
    pairs = []
    for z in range(2):
        for x in range(4):
            for slab in range(16):
                target = (z + dz) % 2 * 4 + (x + dx) % 4
                pairs.append(((z * 4 + x) * 16 + slab, target * 16 + slab))
    return pairs


def band_sum(orbitals, occupation):
    rank = lax.axis_index("band")
    start = jnp.stack([rank // 4, rank % 4]).astype(jnp.int32)

    def send(values, dx, dz):
        return lax.ppermute(values, axes, ring(dx, dz))

    far0, far1, cross0 = partial_densities(
        orbitals, occupation, start, [[(0, 2, 0)], [(0, 2, 1)], [(1, 2, 1), (1, 1, 1)]], "density_0"
    )
    far0 = send(far0, 1, 0)
    far1 = send(far1, -1, 0)
    cross0 = send(cross0, 0, 1)
    right1, left0, cross1 = partial_densities(
        orbitals, occupation, start, [[(0, 1, 1)], [(0, 3, 0)], [(1, 3, 1), (1, 0, 1)]], "density_1"
    )
    from_left1 = send(right1, 1, 0)
    from_right0 = send(left0, -1, 0)
    cross1 = send(cross1, 0, 1)
    right0, left1, own0, own1, line2, line1, line3, line0 = partial_densities(
        orbitals,
        occupation,
        start,
        [[(0, 1, 0)], [(0, 3, 1)], [(0, 0, 0)], [(0, 0, 1)], [(1, 2, 0)], [(1, 1, 0)], [(1, 3, 0)], [(1, 0, 0)]],
        "density_2",
    )
    from_left0 = send(right0 + far0, 1, 0)
    from_right1 = send(left1 + far1, -1, 0)
    lines2 = send(line2 + cross0[0], 2, 0)
    lines1 = send(line1 + cross0[1], 1, 0)
    lines3 = send(line3 + cross1[0], -1, 0)
    other = send(own1 + from_left1 + from_right1, 0, 1)
    upper = ((own0 + from_left0) + from_right0) + other
    lower = ((line0 + cross1[1]) + lines1) + (lines2 + lines3)
    return upper, lower


def solution(mesh):
    in_specs = (P("band", "slab", None, None), P("band"))
    out_specs = (P("slab", "band", None), P("slab", "band", None))
    return jax.shard_map(
        per_device, mesh=mesh, in_specs=in_specs, out_specs=out_specs, check_vma=False
    )
```

```python
import math

import jax
import jax.numpy as jnp
import numpy as np
from jax import lax
from jax.experimental import pallas as pl
from jax.experimental.pallas import tpu as pltpu
from jax.sharding import PartitionSpec as P


spacing = 0.08
axes = ("band", "slab")
piece_bytes = 512 << 10
spare_bytes = 4 << 20


def circle_tables(count):
    quarter = count // 4
    eighth = np.sin(2.0 * np.pi * np.arange(quarter + 1) / count)
    eighth[quarter] = 1.0
    first = np.concatenate([eighth[:quarter], eighth[:0:-1]])
    sine = np.concatenate([first, -first])
    cosine = np.roll(sine, -quarter)
    return cosine, sine


def split_table(table):
    high = table.astype(jnp.bfloat16)
    low = (table - high.astype(np.float64)).astype(jnp.bfloat16)
    return high, low


def dft_tables(count):
    cosine, sine = circle_tables(count)
    phases = np.arange(count)[:, None] * np.arange(count)[None, :] % count
    return cosine[phases], sine[phases]


def line_tables(count):
    cosine, sine = dft_tables(count)
    half = count // 2
    real_rows = cosine[:half].copy()
    imag_rows = -sine[:half]
    imag_rows[0] = cosine[half]
    return real_rows, imag_rows


def split(values):
    high = values.astype(jnp.bfloat16)
    low = (values - high.astype(jnp.float32)).astype(jnp.bfloat16)
    return high, low


def dot3(left, right, dims):
    def one(a, b):
        return lax.dot_general(a, b, (dims, ((), ())), preferred_element_type=jnp.float32)

    return one(left[0], right[0]) + (one(left[1], right[0]) + one(left[0], right[1]))


plain = ((1,), (0,))
rows_rows = ((1,), (1,))


def swap_blocks(parts):
    lane = lax.broadcasted_iota(jnp.int32, parts[0].shape, len(parts[0].shape) - 1)
    axis = len(parts[0].shape) - 1
    even = (lane // 32) % 2 == 0
    low = lane < 64
    pairs = []
    for first, second in ((parts[0], parts[1]), (parts[2], parts[3])):
        pairs.append(
            (
                jnp.where(even, first, pltpu.roll(second, 32, axis)),
                jnp.where(even, pltpu.roll(first, 96, axis), second),
            )
        )
    (a0, a1), (b0, b1) = pairs
    return (
        jnp.where(low, a0, pltpu.roll(b0, 64, axis)),
        jnp.where(low, a1, pltpu.roll(b1, 64, axis)),
        jnp.where(low, pltpu.roll(a0, 64, axis), b0),
        jnp.where(low, pltpu.roll(a1, 64, axis), b1),
    )


def forward_kernel(upper_ref, lower_ref, rh_ref, rl_ref, ih_ref, il_ref, out_ref):
    rows = jnp.concatenate([half[zq] for zq in range(8) for half in (upper_ref, lower_ref)], axis=0)
    mean = jnp.sum(rows) * (1.0 / rows.size)
    operand = split(rows - mean)
    real = dot3((rh_ref[...], rl_ref[...]), operand, rows_rows)
    zero = lax.broadcasted_iota(jnp.int32, real.shape, 0) == 0
    real = real + jnp.where(zero, mean * rows.shape[1], 0.0)
    imag = dot3((ih_ref[...], il_ref[...]), operand, rows_rows)
    low = lax.broadcasted_iota(jnp.int32, (128, 128), 1) < 64
    for pair in range(4):
        a = real[:, pair * 128 : (pair + 1) * 128]
        b = imag[:, pair * 128 : (pair + 1) * 128]
        out_ref[:, 2 * pair, :] = jnp.where(low, a, pltpu.roll(b, 64, 1))
        out_ref[:, 2 * pair + 1, :] = jnp.where(low, pltpu.roll(a, 64, 1), b)


def plane_kernel(freq_ref, message_ref, ch_ref, cl_ref, sh_ref, sl_ref, out_ref):
    count = 256
    cosine = (ch_ref[...], cl_ref[...])
    sine = (sh_ref[...], sl_ref[...])
    columns = [[], []]
    for group in range(2):
        parts = [
            message_ref[(group * 4 + member) * 16 : (group * 4 + member + 1) * 16]
            for member in range(4)
        ]
        blocks = swap_blocks(parts)
        for part in range(2):
            whole = jnp.stack([blocks[part * 2], blocks[part * 2 + 1]], axis=1)
            columns[part].append(whole.reshape(count, 128))
    planes = [jnp.concatenate(columns[part], axis=1) for part in range(2)]
    means = [jnp.sum(part) * (1.0 / count**2) for part in planes]
    operand = split(jnp.concatenate([part - mean for part, mean in zip(planes, means)], axis=0))
    by_cos = dot3(operand, cosine, plain)
    by_sin = dot3(operand, sine, plain)
    real = by_cos[:count] + by_sin[count:]
    imag = by_cos[count:] - by_sin[:count]
    operand = split(jnp.concatenate([real, imag], axis=1))
    by_cos = dot3(cosine, operand, plain)
    by_sin = dot3(sine, operand, plain)
    real = by_cos[:, :count] + by_sin[:, count:]
    imag = by_cos[:, count:] - by_sin[:, :count]

    def signed(axis):
        index = lax.broadcasted_iota(jnp.int32, (count, count), axis)
        return jnp.where(index < count // 2, index, index - count).astype(jnp.float32)

    freq_z = signed(0)
    freq_x = signed(1)
    plane_sq = freq_z * freq_z + freq_x * freq_x
    zero = plane_sq == 0.0
    real = real + jnp.where(zero, means[0] * count**2, 0.0)
    imag = imag + jnp.where(zero, means[1] * count**2, 0.0)
    scale = (2.0 * math.pi / (count * spacing)) ** 2

    def green(freq_y):
        wave_sq = scale * (plane_sq + freq_y * freq_y)
        anchor = wave_sq == 0.0
        return jnp.where(
            anchor, 0.0, (4.0 * math.pi / count**3) / (wave_sq + anchor.astype(jnp.float32))
        )

    green_a = green(freq_ref[0])
    green_b = green(freq_ref[1])
    operand = split(
        jnp.concatenate([real * green_a, imag * green_a, real * green_b, imag * green_b], axis=1)
    )
    by_cos = dot3(cosine, operand, plain)
    by_sin = dot3(sine, operand, plain)
    real_a = by_cos[:, :count] - by_sin[:, count : 2 * count]
    imag_a = by_cos[:, count : 2 * count] + by_sin[:, :count]
    real_b = by_cos[:, 2 * count : 3 * count] - by_sin[:, 3 * count :]
    imag_b = by_cos[:, 3 * count :] + by_sin[:, 2 * count : 3 * count]
    result = dot3(split(jnp.concatenate([real_a, imag_b], axis=0)), cosine, plain) + dot3(
        split(jnp.concatenate([-imag_a, real_b], axis=0)), sine, plain
    )
    for group in range(2):
        blocks = []
        for part in range(2):
            whole = result[part * count : (part + 1) * count, group * 128 : (group + 1) * 128]
            whole = whole.reshape(16, 2, 8, 128)
            blocks += [whole[:, 0], whole[:, 1]]
        for member, values in enumerate(swap_blocks(blocks)):
            out_ref[(group * 4 + member) * 16 : (group * 4 + member + 1) * 16] = values


def inverse_kernel(message_ref, rh_ref, rl_ref, ih_ref, il_ref, out_ref):
    real_table = (rh_ref[...], rl_ref[...])
    imag_table = (ih_ref[...], il_ref[...])
    for zq in range(8):
        rows = message_ref[:, zq, :].T
        real = dot3(split(rows[:64]), real_table, plain)
        imag = dot3(split(rows[64:]), imag_table, plain)
        lines = real + imag
        out_ref[zq] = lines[:32]
        out_ref[zq + 8] = lines[32:]


def density_kernel(pieces, occupation_ref, orbitals_ref, *refs):
    outs, (buffer, weights_ref, sems) = refs[:-3], refs[-3:]
    flat = [piece for group in pieces for piece in group]
    copies = []
    rank = lax.axis_index("band")
    for slot, (half, dx, dz) in enumerate(flat):
        block = (rank + 4 * dz) // 4 % 2 * 4 + (rank + dx) % 4
        source = orbitals_ref.at[:, pl.ds(half * 8, 8), pl.ds(block * 32, 32), :]
        copies.append(pltpu.make_async_copy(source, buffer.at[slot], sems.at[slot]))
    weigh = pltpu.make_async_copy(occupation_ref, weights_ref, sems.at[len(flat)])
    for copy in [weigh, *copies]:
        copy.start()
    weigh.wait()
    weights = [weights_ref[band] for band in range(4)]
    slot = 0
    for out, group in zip(outs, pieces):
        for place in range(len(group)):
            copies[slot].wait()
            total = None
            for band in range(4):
                values = buffer[slot, band].astype(jnp.float32)
                term = values * values * weights[band]
                total = term if total is None else total + term
            if len(group) == 1:
                out[...] = total
            else:
                out[place] = total
            slot += 1


def partial_densities(orbitals, occupation, pieces):
    shapes = [
        pltpu.VMEM((8, 32, 256) if len(g) == 1 else (len(g), 8, 32, 256), jnp.float32)
        for g in pieces
    ]
    count = sum(len(g) for g in pieces)
    limit = count * piece_bytes * 2 + spare_bytes
    return pl.pallas_call(
        lambda *refs: density_kernel(pieces, *refs),
        out_shape=shapes,
        in_specs=[pl.BlockSpec(memory_space=pltpu.HBM)] * 2,
        out_specs=[pl.BlockSpec(memory_space=pltpu.VMEM)] * len(shapes),
        scratch_shapes=[
            pltpu.VMEM((count, 4, 8, 32, 256), jnp.bfloat16),
            pltpu.SMEM((4,), jnp.float32),
            pltpu.SemaphoreType.DMA((count + 1,)),
        ],
        compiler_params=pltpu.CompilerParams(vmem_limit_bytes=limit),
    )(*[pltpu.with_memory_space_constraint(value, pltpu.HBM) for value in (occupation, orbitals)])


def vmem_call(kernel, out_shape, limit, operands, scalars=0):
    placed = [pltpu.with_memory_space_constraint(value, pltpu.VMEM) for value in operands[scalars:]]
    vmem = pl.BlockSpec(memory_space=pltpu.VMEM)
    return pl.pallas_call(
        kernel,
        out_shape=out_shape,
        in_specs=[pl.BlockSpec(memory_space=pltpu.SMEM)] * scalars + [vmem] * len(placed),
        out_specs=jax.tree.map(lambda shape: vmem, out_shape),
        compiler_params=pltpu.CompilerParams(vmem_limit_bytes=limit),
    )(*operands[:scalars], *placed)


def solve(orbitals, occupation):
    count = orbitals.shape[2]
    half = count // 2
    upper, lower = band_sum(orbitals, occupation)

    forward_real, forward_imag = line_tables(count)
    tables = [*split_table(forward_real), *split_table(forward_imag)]
    block = jax.ShapeDtypeStruct((16, 32, count), jnp.float32)
    exchanged = pltpu.VMEM((half, 8, 128), jnp.float32)
    message = vmem_call(forward_kernel, exchanged, 12 << 20, (upper, lower, *tables))
    density = jnp.concatenate([upper, lower], axis=0)
    message = lax.all_to_all(message, axes, 0, 0, tiled=True)

    rank = lax.axis_index("band") * lax.axis_size("slab") + lax.axis_index("slab")
    freq = jnp.stack([rank, jnp.where(rank == 0, half, rank)]).astype(jnp.float32)
    cosine, sine = dft_tables(count)
    tables = [*split_table(cosine), *split_table(sine)]
    message = vmem_call(plane_kernel, exchanged, 24 << 20, (freq, message, *tables), 1)
    message = lax.all_to_all(message, axes, 0, 0, tiled=True)

    weight = np.full((half, 1), 2.0)
    weight[0] = 1.0
    tables = [*split_table(forward_real * weight), *split_table(forward_imag * weight)]
    potential = vmem_call(inverse_kernel, block, 12 << 20, (message, *tables))
    return density, potential


def ring(dx, dz):
    pairs = []
    for z in range(2):
        for x in range(4):
            for slab in range(16):
                target = (z + dz) % 2 * 4 + (x + dx) % 4
                pairs.append(((z * 4 + x) * 16 + slab, target * 16 + slab))
    return pairs


def band_sum(orbitals, occupation):
    def send(values, dx, dz):
        return lax.ppermute(values, axes, ring(dx, dz))

    far0, far1, cross0 = partial_densities(orbitals, occupation, [[(0, 2, 0)], [(0, 2, 1)], [(1, 2, 1), (1, 1, 1)]])
    far0 = send(far0, 1, 0)
    far1 = send(far1, -1, 0)
    cross0 = send(cross0, 0, 1)
    right1, left0, cross1 = partial_densities(orbitals, occupation, [[(0, 1, 1)], [(0, 3, 0)], [(1, 3, 1), (1, 0, 1)]])
    from_left1 = send(right1, 1, 0)
    from_right0 = send(left0, -1, 0)
    cross1 = send(cross1, 0, 1)
    right0, left1, own0, own1, line2, line1, line3, line0 = partial_densities(
        orbitals,
        occupation,
        [[(0, 1, 0)], [(0, 3, 1)], [(0, 0, 0)], [(0, 0, 1)], [(1, 2, 0)], [(1, 1, 0)], [(1, 3, 0)], [(1, 0, 0)]],
    )
    from_left0 = send(right0 + far0, 1, 0)
    from_right1 = send(left1 + far1, -1, 0)
    lines2 = send(line2 + cross0[0], 2, 0)
    lines1 = send(line1 + cross0[1], 1, 0)
    lines3 = send(line3 + cross1[0], -1, 0)
    other = send(own1 + from_left1 + from_right1, 0, 1)
    upper = ((own0 + from_left0) + from_right0) + other
    lower = ((line0 + cross1[1]) + lines1) + (lines2 + lines3)
    return upper, lower


def solution(mesh):
    in_specs = (P("band", "slab", None, None), P("band"))
    out_specs = (P("slab", "band", None), P("slab", "band", None))
    return jax.shard_map(solve, mesh=mesh, in_specs=in_specs, out_specs=out_specs, check_vma=False)
```

```python
import math

import jax
import jax.numpy as jnp
import numpy as np
from jax import lax
from jax.experimental import pallas as pl
from jax.experimental.pallas import tpu as pltpu
from jax.sharding import PartitionSpec as P


spacing = 0.08
axes = ("band", "slab")
piece_bytes = 512 << 10
spare_bytes = 4 << 20


def circle_tables(count):
    quarter = count // 4
    eighth = np.sin(2.0 * np.pi * np.arange(quarter + 1) / count)
    eighth[quarter] = 1.0
    first = np.concatenate([eighth[:quarter], eighth[:0:-1]])
    sine = np.concatenate([first, -first])
    cosine = np.roll(sine, -quarter)
    return cosine, sine


def split_table(table):
    high = table.astype(jnp.bfloat16)
    low = (table - high.astype(np.float64)).astype(jnp.bfloat16)
    return high, low


def dft_tables(count):
    cosine, sine = circle_tables(count)
    phases = np.arange(count)[:, None] * np.arange(count)[None, :] % count
    return cosine[phases], sine[phases]


def line_tables(count):
    cosine, sine = dft_tables(count)
    half = count // 2
    real_rows = cosine[:half].copy()
    imag_rows = -sine[:half]
    imag_rows[0] = cosine[half]
    return real_rows, imag_rows


def split(values):
    high = values.astype(jnp.bfloat16)
    low = (values - high.astype(jnp.float32)).astype(jnp.bfloat16)
    return high, low


def dot3(left, right, dims):
    first = jnp.concatenate([left[0], left[1], left[0]], axis=dims[0][0])
    second = jnp.concatenate([right[0], right[0], right[1]], axis=dims[1][0])
    return lax.dot_general(
        first, second, (dims, ((), ())), preferred_element_type=jnp.float32
    )


plain = ((1,), (0,))
rows_rows = ((1,), (1,))


def swap_blocks(parts):
    lane = lax.broadcasted_iota(jnp.int32, parts[0].shape, len(parts[0].shape) - 1)
    axis = len(parts[0].shape) - 1
    even = (lane // 32) % 2 == 0
    low = lane < 64
    pairs = []
    for first, second in ((parts[0], parts[1]), (parts[2], parts[3])):
        pairs.append(
            (
                jnp.where(even, first, pltpu.roll(second, 32, axis)),
                jnp.where(even, pltpu.roll(first, 96, axis), second),
            )
        )
    (a0, a1), (b0, b1) = pairs
    return (
        jnp.where(low, a0, pltpu.roll(b0, 64, axis)),
        jnp.where(low, a1, pltpu.roll(b1, 64, axis)),
        jnp.where(low, pltpu.roll(a0, 64, axis), b0),
        jnp.where(low, pltpu.roll(a1, 64, axis), b1),
    )


def forward_kernel(upper_ref, lower_ref, high_ref, low_ref, out_ref):
    rows = jnp.concatenate([half[zq] for zq in range(8) for half in (upper_ref, lower_ref)], axis=0)
    mean = jnp.sum(rows) * (1.0 / rows.size)
    lines = dot3((high_ref[...], low_ref[...]), split(rows - mean), rows_rows)
    zero = lax.broadcasted_iota(jnp.int32, (128, 512), 0) == 0
    real = lines[:128] + jnp.where(zero, mean * rows.shape[1], 0.0)
    imag = lines[128:]
    low = lax.broadcasted_iota(jnp.int32, (128, 128), 1) < 64
    for pair in range(4):
        a = real[:, pair * 128 : (pair + 1) * 128]
        b = imag[:, pair * 128 : (pair + 1) * 128]
        out_ref[:, 2 * pair, :] = jnp.where(low, a, pltpu.roll(b, 64, 1))
        out_ref[:, 2 * pair + 1, :] = jnp.where(low, pltpu.roll(a, 64, 1), b)


def plane_kernel(freq_ref, message_ref, high_ref, low_ref, out_ref):
    count = 256
    stacked = (high_ref[...], low_ref[...])
    beside = [jnp.concatenate([table[:count], table[count:]], axis=1) for table in stacked]
    columns = [[], []]
    for group in range(2):
        parts = [
            message_ref[(group * 4 + member) * 16 : (group * 4 + member + 1) * 16]
            for member in range(4)
        ]
        blocks = swap_blocks(parts)
        for part in range(2):
            whole = jnp.stack([blocks[part * 2], blocks[part * 2 + 1]], axis=1)
            columns[part].append(whole.reshape(count, 128))
    planes = [jnp.concatenate(columns[part], axis=1) for part in range(2)]
    means = [jnp.sum(part) * (1.0 / count**2) for part in planes]
    operand = split(jnp.concatenate([part - mean for part, mean in zip(planes, means)], axis=0))
    both = dot3(operand, beside, plain)
    by_cos, by_sin = both[:, :count], both[:, count:]
    real = by_cos[:count] + by_sin[count:]
    imag = by_cos[count:] - by_sin[:count]
    operand = split(jnp.concatenate([real, imag], axis=1))
    both = dot3(stacked, operand, plain)
    by_cos, by_sin = both[:count], both[count:]
    real = by_cos[:, :count] + by_sin[:, count:]
    imag = by_cos[:, count:] - by_sin[:, :count]

    def signed(axis):
        index = lax.broadcasted_iota(jnp.int32, (count, count), axis)
        return jnp.where(index < count // 2, index, index - count).astype(jnp.float32)

    freq_z = signed(0)
    freq_x = signed(1)
    plane_sq = freq_z * freq_z + freq_x * freq_x
    zero = plane_sq == 0.0
    real = real + jnp.where(zero, means[0] * count**2, 0.0)
    imag = imag + jnp.where(zero, means[1] * count**2, 0.0)
    scale = (2.0 * math.pi / (count * spacing)) ** 2

    def green(freq_y):
        wave_sq = scale * (plane_sq + freq_y * freq_y)
        anchor = wave_sq == 0.0
        return jnp.where(
            anchor, 0.0, (4.0 * math.pi / count**3) / (wave_sq + anchor.astype(jnp.float32))
        )

    green_a = green(freq_ref[0])
    green_b = green(freq_ref[1])
    operand = split(
        jnp.concatenate([real * green_a, imag * green_a, real * green_b, imag * green_b], axis=1)
    )
    both = dot3(stacked, operand, plain)
    by_cos, by_sin = both[:count], both[count:]
    real_a = by_cos[:, :count] - by_sin[:, count : 2 * count]
    imag_a = by_cos[:, count : 2 * count] + by_sin[:, :count]
    real_b = by_cos[:, 2 * count : 3 * count] - by_sin[:, 3 * count :]
    imag_b = by_cos[:, 3 * count :] + by_sin[:, 2 * count : 3 * count]
    pair = jnp.concatenate(
        [
            jnp.concatenate([real_a, -imag_a], axis=1),
            jnp.concatenate([imag_b, real_b], axis=1),
        ],
        axis=0,
    )
    result = dot3(split(pair), stacked, plain)
    for group in range(2):
        blocks = []
        for part in range(2):
            whole = result[part * count : (part + 1) * count, group * 128 : (group + 1) * 128]
            whole = whole.reshape(16, 2, 8, 128)
            blocks += [whole[:, 0], whole[:, 1]]
        for member, values in enumerate(swap_blocks(blocks)):
            out_ref[(group * 4 + member) * 16 : (group * 4 + member + 1) * 16] = values


def inverse_kernel(message_ref, high_ref, low_ref, out_ref):
    turned = [message_ref[:, zq, :].T for zq in range(8)]
    rows = jnp.concatenate(
        [jnp.concatenate([block[:64] for block in turned], axis=0),
         jnp.concatenate([block[64:] for block in turned], axis=0)], axis=1
    )
    lines = dot3(split(rows), (high_ref[...], low_ref[...]), plain)
    for zq in range(8):
        out_ref[zq] = lines[zq * 64 : zq * 64 + 32]
        out_ref[zq + 8] = lines[zq * 64 + 32 : zq * 64 + 64]


def density_kernel(pieces, occupation_ref, orbitals_ref, *refs):
    outs, (buffer, weights_ref, sems) = refs[:-3], refs[-3:]
    flat = [piece for group in pieces for piece in group]
    copies = []
    rank = lax.axis_index("band")
    for slot, (half, dx, dz) in enumerate(flat):
        block = (rank + 4 * dz) // 4 % 2 * 4 + (rank + dx) % 4
        source = orbitals_ref.at[:, pl.ds(half * 8, 8), pl.ds(block * 32, 32), :]
        copies.append(pltpu.make_async_copy(source, buffer.at[slot], sems.at[slot]))
    weigh = pltpu.make_async_copy(occupation_ref, weights_ref, sems.at[len(flat)])
    for copy in [weigh, *copies]:
        copy.start()
    weigh.wait()
    weights = [weights_ref[band] for band in range(4)]
    slot = 0
    for out, group in zip(outs, pieces):
        for place in range(len(group)):
            copies[slot].wait()
            total = None
            for band in range(4):
                values = buffer[slot, band].astype(jnp.float32)
                term = values * values * weights[band]
                total = term if total is None else total + term
            if len(group) == 1:
                out[...] = total
            else:
                out[place] = total
            slot += 1


def partial_densities(orbitals, occupation, pieces):
    shapes = [
        pltpu.VMEM((8, 32, 256) if len(g) == 1 else (len(g), 8, 32, 256), jnp.float32)
        for g in pieces
    ]
    count = sum(len(g) for g in pieces)
    limit = count * piece_bytes * 2 + spare_bytes
    return pl.pallas_call(
        lambda *refs: density_kernel(pieces, *refs),
        out_shape=shapes,
        in_specs=[pl.BlockSpec(memory_space=pltpu.HBM)] * 2,
        out_specs=[pl.BlockSpec(memory_space=pltpu.VMEM)] * len(shapes),
        scratch_shapes=[
            pltpu.VMEM((count, 4, 8, 32, 256), jnp.bfloat16),
            pltpu.SMEM((4,), jnp.float32),
            pltpu.SemaphoreType.DMA((count + 1,)),
        ],
        compiler_params=pltpu.CompilerParams(vmem_limit_bytes=limit),
    )(*[pltpu.with_memory_space_constraint(value, pltpu.HBM) for value in (occupation, orbitals)])


def vmem_call(kernel, out_shape, limit, operands, scalars=0):
    placed = [pltpu.with_memory_space_constraint(value, pltpu.VMEM) for value in operands[scalars:]]
    vmem = pl.BlockSpec(memory_space=pltpu.VMEM)
    return pl.pallas_call(
        kernel,
        out_shape=out_shape,
        in_specs=[pl.BlockSpec(memory_space=pltpu.SMEM)] * scalars + [vmem] * len(placed),
        out_specs=jax.tree.map(lambda shape: vmem, out_shape),
        compiler_params=pltpu.CompilerParams(vmem_limit_bytes=limit),
    )(*operands[:scalars], *placed)


def solve(orbitals, occupation):
    count = orbitals.shape[2]
    half = count // 2
    upper, lower = band_sum(orbitals, occupation)

    forward_real, forward_imag = line_tables(count)
    tables = split_table(np.concatenate([forward_real, forward_imag]))
    block = jax.ShapeDtypeStruct((16, 32, count), jnp.float32)
    exchanged = pltpu.VMEM((half, 8, 128), jnp.float32)
    message = vmem_call(forward_kernel, exchanged, 12 << 20, (upper, lower, *tables))
    density = jnp.concatenate([upper, lower], axis=0)
    message = lax.all_to_all(message, axes, 0, 0, tiled=True)

    rank = lax.axis_index("band") * lax.axis_size("slab") + lax.axis_index("slab")
    freq = jnp.stack([rank, jnp.where(rank == 0, half, rank)]).astype(jnp.float32)
    cosine, sine = dft_tables(count)
    tables = split_table(np.concatenate([cosine, sine]))
    message = vmem_call(plane_kernel, exchanged, 24 << 20, (freq, message, *tables), 1)
    message = lax.all_to_all(message, axes, 0, 0, tiled=True)

    weight = np.full((half, 1), 2.0)
    weight[0] = 1.0
    tables = split_table(np.concatenate([forward_real * weight, forward_imag * weight]))
    potential = vmem_call(inverse_kernel, block, 12 << 20, (message, *tables))
    return density, potential


def ring(dx, dz):
    pairs = []
    for z in range(2):
        for x in range(4):
            for slab in range(16):
                target = (z + dz) % 2 * 4 + (x + dx) % 4
                pairs.append(((z * 4 + x) * 16 + slab, target * 16 + slab))
    return pairs


def band_sum(orbitals, occupation):
    def send(values, dx, dz):
        return lax.ppermute(values, axes, ring(dx, dz))

    far0, far1, cross0 = partial_densities(orbitals, occupation, [[(0, 2, 0)], [(0, 2, 1)], [(1, 2, 1), (1, 1, 1)]])
    far0 = send(far0, 1, 0)
    far1 = send(far1, -1, 0)
    cross0 = send(cross0, 0, 1)
    right1, left0, cross1 = partial_densities(orbitals, occupation, [[(0, 1, 1)], [(0, 3, 0)], [(1, 3, 1), (1, 0, 1)]])
    from_left1 = send(right1, 1, 0)
    from_right0 = send(left0, -1, 0)
    cross1 = send(cross1, 0, 1)
    right0, left1, own0, own1, line2, line1, line3, line0 = partial_densities(
        orbitals,
        occupation,
        [[(0, 1, 0)], [(0, 3, 1)], [(0, 0, 0)], [(0, 0, 1)], [(1, 2, 0)], [(1, 1, 0)], [(1, 3, 0)], [(1, 0, 0)]],
    )
    from_left0 = send(right0 + far0, 1, 0)
    from_right1 = send(left1 + far1, -1, 0)
    line2 = line2 + cross0[0]
    ahead = send(line2[:4], 1, 0)
    behind = send(line2[4:], -1, 0)
    line1 = line1 + cross0[1]
    lines1 = send(lax.dynamic_update_slice(line1, line1[:4] + ahead, (0, 0, 0)), 1, 0)
    line3 = line3 + cross1[0]
    lines3 = send(lax.dynamic_update_slice(line3, line3[4:] + behind, (4, 0, 0)), -1, 0)
    other = send(own1 + from_left1 + from_right1, 0, 1)
    upper = ((own0 + from_left0) + from_right0) + other
    lower = (line0 + cross1[1]) + (lines1 + lines3)
    return upper, lower


def solution(mesh):
    in_specs = (P("band", "slab", None, None), P("band"))
    out_specs = (P("slab", "band", None), P("slab", "band", None))
    return jax.shard_map(solve, mesh=mesh, in_specs=in_specs, out_specs=out_specs, check_vma=False)
```

```python
import math

import jax
import jax.numpy as jnp
import numpy as np
from jax import lax
from jax.experimental import pallas as pl
from jax.experimental.pallas import tpu as pltpu
from jax.sharding import PartitionSpec as P


spacing = 0.08
axes = ("band", "slab")
planes = (9, 7)
piece_bytes = 576 << 10
spare_bytes = 4 << 20


def circle_tables(count):
    quarter = count // 4
    eighth = np.sin(2.0 * np.pi * np.arange(quarter + 1) / count)
    eighth[quarter] = 1.0
    first = np.concatenate([eighth[:quarter], eighth[:0:-1]])
    sine = np.concatenate([first, -first])
    cosine = np.roll(sine, -quarter)
    return cosine, sine


def split_table(table):
    high = table.astype(jnp.bfloat16)
    low = (table - high.astype(np.float64)).astype(jnp.bfloat16)
    return high, low


def dft_tables(count):
    cosine, sine = circle_tables(count)
    phases = np.arange(count)[:, None] * np.arange(count)[None, :] % count
    return cosine[phases], sine[phases]


def line_tables(count):
    cosine, sine = dft_tables(count)
    half = count // 2
    real_rows = cosine[:half].copy()
    imag_rows = -sine[:half]
    imag_rows[0] = cosine[half]
    return real_rows, imag_rows


def split(values):
    high = values.astype(jnp.bfloat16)
    low = (values - high.astype(jnp.float32)).astype(jnp.bfloat16)
    return high, low


def dot3(left, right, dims):
    first = jnp.concatenate([left[0], left[1], left[0]], axis=dims[0][0])
    second = jnp.concatenate([right[0], right[0], right[1]], axis=dims[1][0])
    return lax.dot_general(
        first, second, (dims, ((), ())), preferred_element_type=jnp.float32
    )


plain = ((1,), (0,))
rows_rows = ((1,), (1,))


def swap_blocks(parts):
    lane = lax.broadcasted_iota(jnp.int32, parts[0].shape, len(parts[0].shape) - 1)
    axis = len(parts[0].shape) - 1
    even = (lane // 32) % 2 == 0
    low = lane < 64
    pairs = []
    for first, second in ((parts[0], parts[1]), (parts[2], parts[3])):
        pairs.append(
            (
                jnp.where(even, first, pltpu.roll(second, 32, axis)),
                jnp.where(even, pltpu.roll(first, 96, axis), second),
            )
        )
    (a0, a1), (b0, b1) = pairs
    return (
        jnp.where(low, a0, pltpu.roll(b0, 64, axis)),
        jnp.where(low, a1, pltpu.roll(b1, 64, axis)),
        jnp.where(low, pltpu.roll(a0, 64, axis), b0),
        jnp.where(low, pltpu.roll(a1, 64, axis), b1),
    )


def forward_kernel(upper_ref, lower_ref, high_ref, low_ref, out_ref):
    cut = planes[0]
    planes_of = [upper_ref[z] if z < cut else lower_ref[z - cut] for z in range(16)]
    rows = jnp.concatenate([planes_of[zh * 8 + zq] for zq in range(8) for zh in range(2)], axis=0)
    mean = jnp.sum(rows) * (1.0 / rows.size)
    lines = dot3((high_ref[...], low_ref[...]), split(rows - mean), rows_rows)
    zero = lax.broadcasted_iota(jnp.int32, (128, 512), 0) == 0
    real = lines[:128] + jnp.where(zero, mean * rows.shape[1], 0.0)
    imag = lines[128:]
    low = lax.broadcasted_iota(jnp.int32, (128, 128), 1) < 64
    for pair in range(4):
        a = real[:, pair * 128 : (pair + 1) * 128]
        b = imag[:, pair * 128 : (pair + 1) * 128]
        out_ref[:, 2 * pair, :] = jnp.where(low, a, pltpu.roll(b, 64, 1))
        out_ref[:, 2 * pair + 1, :] = jnp.where(low, pltpu.roll(a, 64, 1), b)


def plane_kernel(freq_ref, message_ref, high_ref, low_ref, out_ref):
    count = 256
    stacked = (high_ref[...], low_ref[...])
    beside = [jnp.concatenate([table[:count], table[count:]], axis=1) for table in stacked]
    columns = [[], []]
    for group in range(2):
        parts = [
            message_ref[(group * 4 + member) * 16 : (group * 4 + member + 1) * 16]
            for member in range(4)
        ]
        blocks = swap_blocks(parts)
        for part in range(2):
            whole = jnp.stack([blocks[part * 2], blocks[part * 2 + 1]], axis=1)
            columns[part].append(whole.reshape(count, 128))
    planes = [jnp.concatenate(columns[part], axis=1) for part in range(2)]
    means = [jnp.sum(part) * (1.0 / count**2) for part in planes]
    operand = split(jnp.concatenate([part - mean for part, mean in zip(planes, means)], axis=0))
    both = dot3(operand, beside, plain)
    by_cos, by_sin = both[:, :count], both[:, count:]
    real = by_cos[:count] + by_sin[count:]
    imag = by_cos[count:] - by_sin[:count]
    operand = split(jnp.concatenate([real, imag], axis=1))
    both = dot3(stacked, operand, plain)
    by_cos, by_sin = both[:count], both[count:]
    real = by_cos[:, :count] + by_sin[:, count:]
    imag = by_cos[:, count:] - by_sin[:, :count]

    def signed(axis):
        index = lax.broadcasted_iota(jnp.int32, (count, count), axis)
        return jnp.where(index < count // 2, index, index - count).astype(jnp.float32)

    freq_z = signed(0)
    freq_x = signed(1)
    plane_sq = freq_z * freq_z + freq_x * freq_x
    zero = plane_sq == 0.0
    real = real + jnp.where(zero, means[0] * count**2, 0.0)
    imag = imag + jnp.where(zero, means[1] * count**2, 0.0)
    scale = (2.0 * math.pi / (count * spacing)) ** 2

    def green(freq_y):
        wave_sq = scale * (plane_sq + freq_y * freq_y)
        anchor = wave_sq == 0.0
        return jnp.where(
            anchor, 0.0, (4.0 * math.pi / count**3) / (wave_sq + anchor.astype(jnp.float32))
        )

    green_a = green(freq_ref[0])
    green_b = green(freq_ref[1])
    operand = split(
        jnp.concatenate([real * green_a, imag * green_a, real * green_b, imag * green_b], axis=1)
    )
    both = dot3(stacked, operand, plain)
    by_cos, by_sin = both[:count], both[count:]
    real_a = by_cos[:, :count] - by_sin[:, count : 2 * count]
    imag_a = by_cos[:, count : 2 * count] + by_sin[:, :count]
    real_b = by_cos[:, 2 * count : 3 * count] - by_sin[:, 3 * count :]
    imag_b = by_cos[:, 3 * count :] + by_sin[:, 2 * count : 3 * count]
    pair = jnp.concatenate(
        [
            jnp.concatenate([real_a, -imag_a], axis=1),
            jnp.concatenate([imag_b, real_b], axis=1),
        ],
        axis=0,
    )
    result = dot3(split(pair), stacked, plain)
    for group in range(2):
        blocks = []
        for part in range(2):
            whole = result[part * count : (part + 1) * count, group * 128 : (group + 1) * 128]
            whole = whole.reshape(16, 2, 8, 128)
            blocks += [whole[:, 0], whole[:, 1]]
        for member, values in enumerate(swap_blocks(blocks)):
            out_ref[(group * 4 + member) * 16 : (group * 4 + member + 1) * 16] = values


def inverse_kernel(message_ref, high_ref, low_ref, out_ref):
    turned = [message_ref[:, zq, :].T for zq in range(8)]
    rows = jnp.concatenate(
        [jnp.concatenate([block[:64] for block in turned], axis=0),
         jnp.concatenate([block[64:] for block in turned], axis=0)], axis=1
    )
    lines = dot3(split(rows), (high_ref[...], low_ref[...]), plain)
    for zq in range(8):
        out_ref[zq] = lines[zq * 64 : zq * 64 + 32]
        out_ref[zq + 8] = lines[zq * 64 + 32 : zq * 64 + 64]


def density_kernel(pieces, occupation_ref, orbitals_ref, *refs):
    outs, (buffer, weights_ref, sems) = refs[:-3], refs[-3:]
    flat = [piece for group in pieces for piece in group]
    copies = []
    rank = lax.axis_index("band")
    for slot, (half, dx, dz) in enumerate(flat):
        block = (rank + 4 * dz) // 4 % 2 * 4 + (rank + dx) % 4
        depth = planes[half]
        source = orbitals_ref.at[:, pl.ds(half * planes[0], depth), pl.ds(block * 32, 32), :]
        target = buffer.at[slot, :, pl.ds(0, depth)]
        copies.append(pltpu.make_async_copy(source, target, sems.at[slot]))
    weigh = pltpu.make_async_copy(occupation_ref, weights_ref, sems.at[len(flat)])
    for copy in [weigh, *copies]:
        copy.start()
    weigh.wait()
    weights = [weights_ref[band] for band in range(4)]
    slot = 0
    for out, group in zip(outs, pieces):
        for place in range(len(group)):
            copies[slot].wait()
            total = None
            for band in range(4):
                values = buffer[slot, band, : planes[group[place][0]]].astype(jnp.float32)
                term = values * values * weights[band]
                total = term if total is None else total + term
            if len(group) == 1:
                out[...] = total
            else:
                out[place] = total
            slot += 1


def partial_densities(orbitals, occupation, pieces):
    shapes = [
        pltpu.VMEM((len(g),) * (len(g) > 1) + (planes[g[0][0]], 32, 256), jnp.float32)
        for g in pieces
    ]
    count = sum(len(g) for g in pieces)
    limit = count * piece_bytes * 2 + spare_bytes
    return pl.pallas_call(
        lambda *refs: density_kernel(pieces, *refs),
        out_shape=shapes,
        in_specs=[pl.BlockSpec(memory_space=pltpu.HBM)] * 2,
        out_specs=[pl.BlockSpec(memory_space=pltpu.VMEM)] * len(shapes),
        scratch_shapes=[
            pltpu.VMEM((count, 4, max(planes), 32, 256), jnp.bfloat16),
            pltpu.SMEM((4,), jnp.float32),
            pltpu.SemaphoreType.DMA((count + 1,)),
        ],
        compiler_params=pltpu.CompilerParams(vmem_limit_bytes=limit),
    )(*[pltpu.with_memory_space_constraint(value, pltpu.HBM) for value in (occupation, orbitals)])


def vmem_call(kernel, out_shape, limit, operands, scalars=0):
    placed = [pltpu.with_memory_space_constraint(value, pltpu.VMEM) for value in operands[scalars:]]
    vmem = pl.BlockSpec(memory_space=pltpu.VMEM)
    return pl.pallas_call(
        kernel,
        out_shape=out_shape,
        in_specs=[pl.BlockSpec(memory_space=pltpu.SMEM)] * scalars + [vmem] * len(placed),
        out_specs=jax.tree.map(lambda shape: vmem, out_shape),
        compiler_params=pltpu.CompilerParams(vmem_limit_bytes=limit),
    )(*operands[:scalars], *placed)


def solve(orbitals, occupation):
    count = orbitals.shape[2]
    half = count // 2
    upper, lower = band_sum(orbitals, occupation)

    forward_real, forward_imag = line_tables(count)
    tables = split_table(np.concatenate([forward_real, forward_imag]))
    block = jax.ShapeDtypeStruct((16, 32, count), jnp.float32)
    exchanged = pltpu.VMEM((half, 8, 128), jnp.float32)
    message = vmem_call(forward_kernel, exchanged, 12 << 20, (upper, lower, *tables))
    density = jnp.concatenate([upper, lower], axis=0)
    message = lax.all_to_all(message, axes, 0, 0, tiled=True)

    rank = lax.axis_index("band") * lax.axis_size("slab") + lax.axis_index("slab")
    freq = jnp.stack([rank, jnp.where(rank == 0, half, rank)]).astype(jnp.float32)
    cosine, sine = dft_tables(count)
    tables = split_table(np.concatenate([cosine, sine]))
    message = vmem_call(plane_kernel, exchanged, 24 << 20, (freq, message, *tables), 1)
    message = lax.all_to_all(message, axes, 0, 0, tiled=True)

    weight = np.full((half, 1), 2.0)
    weight[0] = 1.0
    tables = split_table(np.concatenate([forward_real * weight, forward_imag * weight]))
    potential = vmem_call(inverse_kernel, block, 12 << 20, (message, *tables))
    return density, potential


def ring(dx, dz):
    pairs = []
    for z in range(2):
        for x in range(4):
            for slab in range(16):
                target = (z + dz) % 2 * 4 + (x + dx) % 4
                pairs.append(((z * 4 + x) * 16 + slab, target * 16 + slab))
    return pairs


def band_sum(orbitals, occupation):
    def send(values, dx, dz):
        return lax.ppermute(values, axes, ring(dx, dz))

    far0, far1, cross0 = partial_densities(orbitals, occupation, [[(0, 2, 0)], [(0, 2, 1)], [(1, 2, 1), (1, 1, 1)]])
    far0 = send(far0, 1, 0)
    far1 = send(far1, -1, 0)
    cross0 = send(cross0, 0, 1)
    right1, left0, cross3, cross4 = partial_densities(
        orbitals, occupation, [[(0, 1, 1)], [(0, 3, 0)], [(1, 3, 1)], [(1, 0, 1)]]
    )
    from_left1 = send(right1, 1, 0)
    from_right0 = send(left0, -1, 0)
    right0, left1, own0, own1, line2, line1, line3, line0 = partial_densities(
        orbitals,
        occupation,
        [[(0, 1, 0)], [(0, 3, 1)], [(0, 0, 0)], [(0, 0, 1)], [(1, 2, 0)], [(1, 1, 0)], [(1, 3, 0)], [(1, 0, 0)]],
    )
    from_left0 = send(right0 + far0, 1, 0)
    from_right1 = send(left1 + far1, -1, 0)
    cross3 = send(cross3, 0, 1)
    cross4 = send(cross4, 0, 1)
    half = planes[1] // 2 + 1
    line2 = line2 + cross0[0]
    ahead = send(line2[:half], 1, 0)
    behind = send(line2[half:], -1, 0)
    line1 = line1 + cross0[1]
    line1 = lax.dynamic_update_slice(line1, line1[:half] + ahead, (0, 0, 0))
    lines1 = send(line1, 1, 0)
    line3 = line3 + cross3
    line3 = lax.dynamic_update_slice(line3, line3[half:] + behind, (half, 0, 0))
    lines3 = send(line3, -1, 0)
    other = send(own1 + from_left1 + from_right1, 0, 1)
    upper = ((own0 + from_left0) + from_right0) + other
    lower = (line0 + cross4) + (lines1 + lines3)
    return upper, lower


def solution(mesh):
    in_specs = (P("band", "slab", None, None), P("band"))
    out_specs = (P("slab", "band", None), P("slab", "band", None))
    return jax.shard_map(solve, mesh=mesh, in_specs=in_specs, out_specs=out_specs, check_vma=False)
```

```python
import math

import jax
import jax.numpy as jnp
import numpy as np
from jax import lax
from jax.experimental import pallas as pl
from jax.experimental.pallas import tpu as pltpu
from jax.sharding import PartitionSpec as P


spacing = 0.08
axes = ("band", "slab")
planes = (9, 7)
piece_bytes = 576 << 10
spare_bytes = 4 << 20


def circle_tables(count):
    quarter = count // 4
    eighth = np.sin(2.0 * np.pi * np.arange(quarter + 1) / count)
    eighth[quarter] = 1.0
    first = np.concatenate([eighth[:quarter], eighth[:0:-1]])
    sine = np.concatenate([first, -first])
    cosine = np.roll(sine, -quarter)
    return cosine, sine


def split_table(table):
    high = table.astype(jnp.bfloat16)
    low = (table - high.astype(np.float64)).astype(jnp.bfloat16)
    return high, low


def dft_tables(count):
    cosine, sine = circle_tables(count)
    phases = np.arange(count)[:, None] * np.arange(count)[None, :] % count
    return cosine[phases], sine[phases]


def line_tables(count):
    cosine, sine = dft_tables(count)
    half = count // 2
    real_rows = cosine[:half].copy()
    imag_rows = -sine[:half]
    imag_rows[0] = cosine[half]
    return real_rows, imag_rows


def split(values):
    high = values.astype(jnp.bfloat16)
    low = (values - high.astype(jnp.float32)).astype(jnp.bfloat16)
    return high, low


def dot3(left, right, dims):
    first = jnp.concatenate([left[0], left[1], left[0]], axis=dims[0][0])
    second = jnp.concatenate([right[0], right[0], right[1]], axis=dims[1][0])
    return lax.dot_general(
        first, second, (dims, ((), ())), preferred_element_type=jnp.float32
    )


plain = ((1,), (0,))
rows_rows = ((1,), (1,))


def swap_blocks(parts):
    lane = lax.broadcasted_iota(jnp.int32, parts[0].shape, len(parts[0].shape) - 1)
    axis = len(parts[0].shape) - 1
    even = (lane // 32) % 2 == 0
    low = lane < 64
    pairs = []
    for first, second in ((parts[0], parts[1]), (parts[2], parts[3])):
        pairs.append(
            (
                jnp.where(even, first, pltpu.roll(second, 32, axis)),
                jnp.where(even, pltpu.roll(first, 96, axis), second),
            )
        )
    results = []
    for first, second in zip(*pairs):
        turned = pltpu.roll(jnp.where(low, second, first), 64, axis)
        results.append((jnp.where(low, first, turned), jnp.where(low, turned, second)))
    return [pair[0] for pair in results] + [pair[1] for pair in results]


def forward_kernel(upper_ref, lower_ref, high_ref, low_ref, out_ref):
    cut = planes[0]
    planes_of = [upper_ref[z] if z < cut else lower_ref[z - cut] for z in range(16)]
    rows = jnp.concatenate([planes_of[zh * 8 + zq] for zq in range(8) for zh in range(2)], axis=0)
    mean = jnp.sum(rows) * (1.0 / rows.size)
    lines = dot3((high_ref[...], low_ref[...]), split(rows - mean), rows_rows)
    zero = lax.broadcasted_iota(jnp.int32, (128, 512), 0) == 0
    real = lines[:128] + jnp.where(zero, mean * rows.shape[1], 0.0)
    imag = lines[128:]
    low = lax.broadcasted_iota(jnp.int32, (128, 128), 1) < 64
    for pair in range(4):
        a = real[:, pair * 128 : (pair + 1) * 128]
        b = imag[:, pair * 128 : (pair + 1) * 128]
        out_ref[pl.ds(2 * pair, 128, stride=8), :] = jnp.where(low, a, pltpu.roll(b, 64, 1))
        out_ref[pl.ds(2 * pair + 1, 128, stride=8), :] = jnp.where(low, pltpu.roll(a, 64, 1), b)


def plane_kernel(green_ref, message_ref, high_ref, low_ref, out_ref):
    count = 256
    stacked = (high_ref[...], low_ref[...])
    beside = [jnp.concatenate([table[:count], table[count:]], axis=1) for table in stacked]
    tile = jnp.sum(message_ref[...].reshape(128, 8, 128), axis=0)
    real_lane = lax.broadcasted_iota(jnp.int32, tile.shape, 1) < 64
    means = [
        jnp.sum(jnp.where(real_lane == keep, tile, 0.0)) * (1.0 / count**2) for keep in (True, False)
    ]
    reals, imags = [], []
    chunks = 1
    slabs = 16 // chunks
    rows = count // chunks
    for chunk in range(chunks):
        columns = [[], []]
        for group in range(2):
            parts = [
                message_ref[pl.ds((member * 16 + chunk * slabs) * 8, slabs * 8), :].reshape(
                    slabs, 8, 128
                )
                for member in range(group * 4, group * 4 + 4)
            ]
            blocks = swap_blocks(parts)
            for part in range(2):
                whole = jnp.stack([blocks[part * 2], blocks[part * 2 + 1]], axis=1)
                columns[part].append(whole.reshape(rows, 128))
        halves = [jnp.concatenate(columns[part], axis=1) - means[part] for part in range(2)]
        both = dot3(split(jnp.concatenate(halves, axis=0)), beside, plain)
        by_cos, by_sin = both[:, :count], both[:, count:]
        reals.append(by_cos[:rows] + by_sin[rows:])
        imags.append(by_cos[rows:] - by_sin[:rows])
    real = jnp.concatenate(reals, axis=0)
    imag = jnp.concatenate(imags, axis=0)
    both = dot3(stacked, split(jnp.concatenate([real, imag], axis=1)), plain)
    by_cos, by_sin = both[:count], both[count:]
    real = by_cos[:, :count] + by_sin[:, count:]
    imag = by_cos[:, count:] - by_sin[:, :count]
    zero = (lax.broadcasted_iota(jnp.int32, (count, count), 0) == 0) & (
        lax.broadcasted_iota(jnp.int32, (count, count), 1) == 0
    )
    real = real + jnp.where(zero, means[0] * count**2, 0.0)
    imag = imag + jnp.where(zero, means[1] * count**2, 0.0)
    green_a = green_ref[0]
    green_b = green_ref[1]
    operand = split(
        jnp.concatenate([real * green_a, imag * green_a, real * green_b, imag * green_b], axis=1)
    )
    both = dot3(stacked, operand, plain)
    by_cos, by_sin = both[:count], both[count:]
    real_a = by_cos[:, :count] - by_sin[:, count : 2 * count]
    imag_a = by_cos[:, count : 2 * count] + by_sin[:, :count]
    real_b = by_cos[:, 2 * count : 3 * count] - by_sin[:, 3 * count :]
    imag_b = by_cos[:, 3 * count :] + by_sin[:, 2 * count : 3 * count]
    for chunk in range(chunks):
        piece = slice(chunk * rows, (chunk + 1) * rows)
        pair = jnp.concatenate(
            [
                jnp.concatenate([real_a[piece], -imag_a[piece]], axis=1),
                jnp.concatenate([imag_b[piece], real_b[piece]], axis=1),
            ],
            axis=0,
        )
        result = dot3(split(pair), stacked, plain)
        for group in range(2):
            blocks = []
            for part in range(2):
                whole = result[part * rows : (part + 1) * rows, group * 128 : (group + 1) * 128]
                whole = whole.reshape(slabs, 2, 8, 128)
                blocks += [whole[:, 0], whole[:, 1]]
            for member, values in enumerate(swap_blocks(blocks), group * 4):
                place = pl.ds((member * 16 + chunk * slabs) * 8, slabs * 8)
                out_ref[place, :] = values.reshape(slabs * 8, 128)


def green_planes(rank, count):
    def signed(axis):
        index = lax.broadcasted_iota(jnp.int32, (2, count, count), axis)
        return jnp.where(index < count // 2, index, index - count).astype(jnp.float32)

    freq_z, freq_x = signed(1), signed(2)
    second = lax.broadcasted_iota(jnp.int32, (2, count, count), 0) == 1
    freq_y = jnp.where(second & (rank == 0), count // 2, rank).astype(jnp.float32)
    scale = (2.0 * math.pi / (count * spacing)) ** 2
    wave_sq = scale * (freq_z * freq_z + freq_x * freq_x + freq_y * freq_y)
    anchor = wave_sq == 0.0
    inverse_points = 1.0 / count**3
    return jnp.where(
        anchor, 0.0, 4.0 * math.pi * inverse_points / (wave_sq + anchor.astype(jnp.float32))
    )


def inverse_kernel(message_ref, high_ref, low_ref, out_ref):
    turned = [message_ref[pl.ds(zq, 128, stride=8), :].T for zq in range(8)]
    rows = jnp.concatenate(
        [jnp.concatenate([block[:64] for block in turned], axis=0),
         jnp.concatenate([block[64:] for block in turned], axis=0)], axis=1
    )
    lines = dot3(split(rows), (high_ref[...], low_ref[...]), plain)
    for zq in range(8):
        out_ref[zq] = lines[zq * 64 : zq * 64 + 32]
        out_ref[zq + 8] = lines[zq * 64 + 32 : zq * 64 + 64]


def density_kernel(pieces, occupation_ref, orbitals_ref, *refs):
    outs, (buffer, weights_ref, sems) = refs[:-3], refs[-3:]
    flat = [piece for group in pieces for piece in group]
    copies = []
    rank = lax.axis_index("band")
    for slot, (half, dx, dz) in enumerate(flat):
        block = (rank + 4 * dz) // 4 % 2 * 4 + (rank + dx) % 4
        depth = planes[half]
        source = orbitals_ref.at[:, pl.ds(half * planes[0], depth), pl.ds(block * 32, 32), :]
        target = buffer.at[slot, :, pl.ds(0, depth)]
        copies.append(pltpu.make_async_copy(source, target, sems.at[slot]))
    weigh = pltpu.make_async_copy(occupation_ref, weights_ref, sems.at[len(flat)])
    for copy in [weigh, *copies]:
        copy.start()
    weigh.wait()
    weights = [weights_ref[band] for band in range(4)]
    slot = 0
    for out, group in zip(outs, pieces):
        for place in range(len(group)):
            copies[slot].wait()
            total = None
            for band in range(4):
                values = buffer[slot, band, : planes[group[place][0]]].astype(jnp.float32)
                term = values * values * weights[band]
                total = term if total is None else total + term
            if len(group) == 1:
                out[...] = total
            else:
                out[place] = total
            slot += 1


def partial_densities(orbitals, occupation, pieces):
    shapes = [
        pltpu.VMEM((len(g),) * (len(g) > 1) + (planes[g[0][0]], 32, 256), jnp.float32)
        for g in pieces
    ]
    count = sum(len(g) for g in pieces)
    limit = count * piece_bytes * 2 + spare_bytes
    return pl.pallas_call(
        lambda *refs: density_kernel(pieces, *refs),
        out_shape=shapes,
        in_specs=[pl.BlockSpec(memory_space=pltpu.HBM)] * 2,
        out_specs=[pl.BlockSpec(memory_space=pltpu.VMEM)] * len(shapes),
        scratch_shapes=[
            pltpu.VMEM((count, 4, max(planes), 32, 256), jnp.bfloat16),
            pltpu.SMEM((4,), jnp.float32),
            pltpu.SemaphoreType.DMA((count + 1,)),
        ],
        compiler_params=pltpu.CompilerParams(vmem_limit_bytes=limit),
    )(*[pltpu.with_memory_space_constraint(value, pltpu.HBM) for value in (occupation, orbitals)])


def vmem_call(kernel, out_shape, limit, operands):
    placed = [pltpu.with_memory_space_constraint(value, pltpu.VMEM) for value in operands]
    vmem = pl.BlockSpec(memory_space=pltpu.VMEM)
    return pl.pallas_call(
        kernel,
        out_shape=out_shape,
        in_specs=[vmem] * len(placed),
        out_specs=jax.tree.map(lambda shape: vmem, out_shape),
        compiler_params=pltpu.CompilerParams(vmem_limit_bytes=limit),
    )(*placed)


def exchange(message):
    return lax.all_to_all(message, axes, 0, 0, tiled=True)


def solve(orbitals, occupation):
    count = orbitals.shape[2]
    half = count // 2
    upper, lower = band_sum(orbitals, occupation)

    forward_real, forward_imag = line_tables(count)
    tables = split_table(np.concatenate([forward_real, forward_imag]))
    block = jax.ShapeDtypeStruct((16, 32, count), jnp.float32)
    exchanged = pltpu.VMEM((half * 8, 128), jnp.float32)
    message = vmem_call(forward_kernel, exchanged, 12 << 20, (upper, lower, *tables))
    density = jnp.concatenate([upper, lower], axis=0)
    rank = lax.axis_index("band") * lax.axis_size("slab") + lax.axis_index("slab")
    rank, message = lax.optimization_barrier((rank, message))
    green = green_planes(rank, count)
    message = exchange(message)
    cosine, sine = dft_tables(count)
    tables = split_table(np.concatenate([cosine, sine]))
    message = vmem_call(plane_kernel, exchanged, 24 << 20, (green, message, *tables))
    message = exchange(message)

    weight = np.full((half, 1), 2.0)
    weight[0] = 1.0
    tables = split_table(np.concatenate([forward_real * weight, forward_imag * weight]))
    potential = vmem_call(inverse_kernel, block, 12 << 20, (message, *tables))
    return density, potential


def ring(dx, dz):
    pairs = []
    for z in range(2):
        for x in range(4):
            for slab in range(16):
                target = (z + dz) % 2 * 4 + (x + dx) % 4
                pairs.append(((z * 4 + x) * 16 + slab, target * 16 + slab))
    return pairs


def band_sum(orbitals, occupation):
    def send(values, dx, dz):
        return lax.ppermute(values, axes, ring(dx, dz))

    far0, far1, cross2 = partial_densities(
        orbitals, occupation, [[(0, 2, 0)], [(0, 2, 1)], [(1, 2, 1)]]
    )
    far0 = send(far0, 1, 0)
    far1 = send(far1, -1, 0)
    cross2 = send(cross2, 0, 1)
    cross1, right1, left0, cross3 = partial_densities(
        orbitals, occupation, [[(1, 1, 1)], [(0, 1, 1)], [(0, 3, 0)], [(1, 3, 1)]]
    )
    cross1 = send(cross1, 0, 1)
    from_left1 = send(right1, 1, 0)
    from_right0 = send(left0, -1, 0)
    left1, right0, line2, cross4, line1, line3, own1, own0, line0 = partial_densities(
        orbitals,
        occupation,
        [
            [(0, 3, 1)],
            [(0, 1, 0)],
            [(1, 2, 0)],
            [(1, 0, 1)],
            [(1, 1, 0)],
            [(1, 3, 0)],
            [(0, 0, 1)],
            [(0, 0, 0)],
            [(1, 0, 0)],
        ],
    )
    from_left0 = send(right0 + far0, 1, 0)
    from_right1 = send(left1 + far1, -1, 0)
    cross3 = send(cross3, 0, 1)
    cross4 = send(cross4, 0, 1)
    half = planes[1] // 2 + 1
    line2 = line2 + cross2
    ahead = send(line2[:half], 1, 0)
    behind = send(line2[half:], -1, 0)
    line1 = line1 + cross1
    line1 = lax.dynamic_update_slice(line1, line1[:half] + ahead, (0, 0, 0))
    lines1 = send(line1, 1, 0)
    line3 = line3 + cross3
    line3 = lax.dynamic_update_slice(line3, line3[half:] + behind, (half, 0, 0))
    lines3 = send(line3, -1, 0)
    other = send(own1 + from_left1 + from_right1, 0, 1)
    upper = ((own0 + from_left0) + from_right0) + other
    lower = (line0 + cross4) + (lines1 + lines3)
    return upper, lower


def solution(mesh):
    in_specs = (P("band", "slab", None, None), P("band"))
    out_specs = (P("slab", "band", None), P("slab", "band", None))
    return jax.shard_map(solve, mesh=mesh, in_specs=in_specs, out_specs=out_specs, check_vma=False)
```

```python
import math

import jax
import jax.numpy as jnp
import numpy as np
from jax import lax
from jax.experimental import pallas as pl
from jax.experimental.pallas import tpu as pltpu
from jax.sharding import PartitionSpec as P


spacing = 0.08
axes = ("band", "slab")
planes = (9, 7)
piece_bytes = 576 << 10
spare_bytes = 4 << 20


def circle_tables(count):
    quarter = count // 4
    eighth = np.sin(2.0 * np.pi * np.arange(quarter + 1) / count)
    eighth[quarter] = 1.0
    first = np.concatenate([eighth[:quarter], eighth[:0:-1]])
    sine = np.concatenate([first, -first])
    cosine = np.roll(sine, -quarter)
    return cosine, sine


def split_table(table):
    high = table.astype(jnp.bfloat16)
    low = (table - high.astype(np.float64)).astype(jnp.bfloat16)
    return high, low


def dft_tables(count):
    cosine, sine = circle_tables(count)
    phases = np.arange(count)[:, None] * np.arange(count)[None, :] % count
    return cosine[phases], sine[phases]


def line_tables(count):
    cosine, sine = dft_tables(count)
    half = count // 2
    real_rows = cosine[:half].copy()
    imag_rows = -sine[:half]
    imag_rows[0] = cosine[half]
    return real_rows, imag_rows


def split(values):
    high = values.astype(jnp.bfloat16)
    low = (values - high.astype(jnp.float32)).astype(jnp.bfloat16)
    return high, low


def dot3(left, right, dims):
    first = jnp.concatenate([left[0], left[1], left[0]], axis=dims[0][0])
    second = jnp.concatenate([right[0], right[0], right[1]], axis=dims[1][0])
    return lax.dot_general(
        first, second, (dims, ((), ())), preferred_element_type=jnp.float32
    )


plain = ((1,), (0,))
rows_rows = ((1,), (1,))


def swap_blocks(parts):
    lane = lax.broadcasted_iota(jnp.int32, parts[0].shape, len(parts[0].shape) - 1)
    axis = len(parts[0].shape) - 1
    even = (lane // 32) % 2 == 0
    low = lane < 64
    pairs = []
    for first, second in ((parts[0], parts[1]), (parts[2], parts[3])):
        pairs.append(
            (
                jnp.where(even, first, pltpu.roll(second, 32, axis)),
                jnp.where(even, pltpu.roll(first, 96, axis), second),
            )
        )
    results = []
    for first, second in zip(*pairs):
        turned = pltpu.roll(jnp.where(low, second, first), 64, axis)
        results.append((jnp.where(low, first, turned), jnp.where(low, turned, second)))
    return [pair[0] for pair in results] + [pair[1] for pair in results]


def forward_kernel(upper_ref, lower_ref, high_ref, low_ref, out_ref):
    cut = planes[0]
    planes_of = [upper_ref[z] if z < cut else lower_ref[z - cut] for z in range(16)]
    rows = jnp.concatenate([planes_of[zh * 8 + zq] for zq in range(8) for zh in range(2)], axis=0)
    mean = jnp.sum(rows) * (1.0 / rows.size)
    lines = dot3((high_ref[...], low_ref[...]), split(rows - mean), rows_rows)
    zero = lax.broadcasted_iota(jnp.int32, (128, 512), 0) == 0
    real = lines[:128] + jnp.where(zero, mean * rows.shape[1], 0.0)
    imag = lines[128:]
    low = lax.broadcasted_iota(jnp.int32, (128, 128), 1) < 64
    for pair in range(4):
        a = real[:, pair * 128 : (pair + 1) * 128]
        b = imag[:, pair * 128 : (pair + 1) * 128]
        out_ref[pl.ds(2 * pair, 128, stride=8), :] = jnp.where(low, a, pltpu.roll(b, 64, 1))
        out_ref[pl.ds(2 * pair + 1, 128, stride=8), :] = jnp.where(low, pltpu.roll(a, 64, 1), b)


def plane_kernel(green_ref, message_ref, high_ref, low_ref, out_ref):
    count = 256
    stacked = (high_ref[...], low_ref[...])
    beside = [jnp.concatenate([table[:count], table[count:]], axis=1) for table in stacked]
    tile = jnp.sum(message_ref[...].reshape(128, 8, 128), axis=0)
    real_lane = lax.broadcasted_iota(jnp.int32, tile.shape, 1) < 64
    means = [
        jnp.sum(jnp.where(real_lane == keep, tile, 0.0)) * (1.0 / count**2) for keep in (True, False)
    ]
    reals, imags = [], []
    chunks = 1
    slabs = 16 // chunks
    rows = count // chunks
    for chunk in range(chunks):
        columns = [[], []]
        for group in range(2):
            parts = [
                message_ref[pl.ds((member * 16 + chunk * slabs) * 8, slabs * 8), :].reshape(
                    slabs, 8, 128
                )
                for member in range(group * 4, group * 4 + 4)
            ]
            blocks = swap_blocks(parts)
            for part in range(2):
                whole = jnp.stack([blocks[part * 2], blocks[part * 2 + 1]], axis=1)
                columns[part].append(whole.reshape(rows, 128))
        halves = [jnp.concatenate(columns[part], axis=1) - means[part] for part in range(2)]
        both = dot3(split(jnp.concatenate(halves, axis=0)), beside, plain)
        by_cos, by_sin = both[:, :count], both[:, count:]
        reals.append(by_cos[:rows] + by_sin[rows:])
        imags.append(by_cos[rows:] - by_sin[:rows])
    real = jnp.concatenate(reals, axis=0)
    imag = jnp.concatenate(imags, axis=0)
    both = dot3(stacked, split(jnp.concatenate([real, imag], axis=1)), plain)
    by_cos, by_sin = both[:count], both[count:]
    real = by_cos[:, :count] + by_sin[:, count:]
    imag = by_cos[:, count:] - by_sin[:, :count]
    zero = (lax.broadcasted_iota(jnp.int32, (count, count), 0) == 0) & (
        lax.broadcasted_iota(jnp.int32, (count, count), 1) == 0
    )
    real = real + jnp.where(zero, means[0] * count**2, 0.0)
    imag = imag + jnp.where(zero, means[1] * count**2, 0.0)
    green_a = green_ref[0]
    green_b = green_ref[1]
    operand = split(
        jnp.concatenate([real * green_a, imag * green_a, real * green_b, imag * green_b], axis=1)
    )
    both = dot3(stacked, operand, plain)
    by_cos, by_sin = both[:count], both[count:]
    real_a = by_cos[:, :count] - by_sin[:, count : 2 * count]
    imag_a = by_cos[:, count : 2 * count] + by_sin[:, :count]
    real_b = by_cos[:, 2 * count : 3 * count] - by_sin[:, 3 * count :]
    imag_b = by_cos[:, 3 * count :] + by_sin[:, 2 * count : 3 * count]
    for chunk in range(chunks):
        piece = slice(chunk * rows, (chunk + 1) * rows)
        pair = jnp.concatenate(
            [
                jnp.concatenate([real_a[piece], -imag_a[piece]], axis=1),
                jnp.concatenate([imag_b[piece], real_b[piece]], axis=1),
            ],
            axis=0,
        )
        result = dot3(split(pair), stacked, plain)
        for group in range(2):
            blocks = []
            for part in range(2):
                whole = result[part * rows : (part + 1) * rows, group * 128 : (group + 1) * 128]
                whole = whole.reshape(slabs, 2, 8, 128)
                blocks += [whole[:, 0], whole[:, 1]]
            for member, values in enumerate(swap_blocks(blocks), group * 4):
                place = pl.ds((member * 16 + chunk * slabs) * 8, slabs * 8)
                out_ref[place, :] = values.reshape(slabs * 8, 128)


def green_kernel(after_ref, out_ref):
    del after_ref
    count = 256
    rank = lax.axis_index("band") * lax.axis_size("slab") + lax.axis_index("slab")

    def signed(axis):
        index = lax.broadcasted_iota(jnp.int32, (count, count), axis)
        return jnp.where(index < count // 2, index, index - count).astype(jnp.float32)

    freq_z, freq_x = signed(0), signed(1)
    scale = (2.0 * math.pi / (count * spacing)) ** 2
    for place, freq in enumerate((rank, jnp.where(rank == 0, count // 2, rank))):
        freq_y = freq.astype(jnp.float32)
        wave_sq = scale * (freq_z * freq_z + freq_x * freq_x + freq_y * freq_y)
        anchor = wave_sq == 0.0
        out_ref[place] = jnp.where(
            anchor, 0.0, (4.0 * math.pi / count**3) / (wave_sq + anchor.astype(jnp.float32))
        )


def inverse_kernel(message_ref, high_ref, low_ref, out_ref):
    turned = [message_ref[pl.ds(zq, 128, stride=8), :].T for zq in range(8)]
    rows = jnp.concatenate(
        [jnp.concatenate([block[:64] for block in turned], axis=0),
         jnp.concatenate([block[64:] for block in turned], axis=0)], axis=1
    )
    lines = dot3(split(rows), (high_ref[...], low_ref[...]), plain)
    for zq in range(8):
        out_ref[zq] = lines[zq * 64 : zq * 64 + 32]
        out_ref[zq + 8] = lines[zq * 64 + 32 : zq * 64 + 64]


def density_kernel(pieces, occupation_ref, orbitals_ref, *refs):
    outs, (buffer, weights_ref, sems) = refs[:-3], refs[-3:]
    flat = [piece for group in pieces for piece in group]
    copies = []
    rank = lax.axis_index("band")
    for slot, (half, dx, dz) in enumerate(flat):
        block = (rank + 4 * dz) // 4 % 2 * 4 + (rank + dx) % 4
        depth = planes[half]
        source = orbitals_ref.at[:, pl.ds(half * planes[0], depth), pl.ds(block * 32, 32), :]
        target = buffer.at[slot, :, pl.ds(0, depth)]
        copies.append(pltpu.make_async_copy(source, target, sems.at[slot]))
    weigh = pltpu.make_async_copy(occupation_ref, weights_ref, sems.at[len(flat)])
    for copy in [weigh, *copies]:
        copy.start()
    weigh.wait()
    weights = [weights_ref[band] for band in range(4)]
    slot = 0
    for out, group in zip(outs, pieces):
        for place in range(len(group)):
            copies[slot].wait()
            total = None
            for band in range(4):
                values = buffer[slot, band, : planes[group[place][0]]].astype(jnp.float32)
                term = values * values * weights[band]
                total = term if total is None else total + term
            if len(group) == 1:
                out[...] = total
            else:
                out[place] = total
            slot += 1


def partial_densities(orbitals, occupation, pieces):
    shapes = [
        pltpu.VMEM((len(g),) * (len(g) > 1) + (planes[g[0][0]], 32, 256), jnp.float32)
        for g in pieces
    ]
    count = sum(len(g) for g in pieces)
    limit = count * piece_bytes * 2 + spare_bytes
    return pl.pallas_call(
        lambda *refs: density_kernel(pieces, *refs),
        out_shape=shapes,
        in_specs=[pl.BlockSpec(memory_space=pltpu.HBM)] * 2,
        out_specs=[pl.BlockSpec(memory_space=pltpu.VMEM)] * len(shapes),
        scratch_shapes=[
            pltpu.VMEM((count, 4, max(planes), 32, 256), jnp.bfloat16),
            pltpu.SMEM((4,), jnp.float32),
            pltpu.SemaphoreType.DMA((count + 1,)),
        ],
        compiler_params=pltpu.CompilerParams(vmem_limit_bytes=limit),
    )(*[pltpu.with_memory_space_constraint(value, pltpu.HBM) for value in (occupation, orbitals)])


def vmem_call(kernel, out_shape, limit, operands):
    placed = [pltpu.with_memory_space_constraint(value, pltpu.VMEM) for value in operands]
    vmem = pl.BlockSpec(memory_space=pltpu.VMEM)
    return pl.pallas_call(
        kernel,
        out_shape=out_shape,
        in_specs=[vmem] * len(placed),
        out_specs=jax.tree.map(lambda shape: vmem, out_shape),
        compiler_params=pltpu.CompilerParams(vmem_limit_bytes=limit),
    )(*placed)


def exchange(message):
    return lax.all_to_all(message, axes, 0, 0, tiled=True)


def solve(orbitals, occupation):
    count = orbitals.shape[2]
    half = count // 2
    upper, lower = band_sum(orbitals, occupation)

    forward_real, forward_imag = line_tables(count)
    tables = split_table(np.concatenate([forward_real, forward_imag]))
    block = jax.ShapeDtypeStruct((16, 32, count), jnp.float32)
    exchanged = pltpu.VMEM((half * 8, 128), jnp.float32)
    message = vmem_call(forward_kernel, exchanged, 12 << 20, (upper, lower, *tables))
    density = jnp.concatenate([upper, lower], axis=0)
    green = pl.pallas_call(
        green_kernel,
        out_shape=pltpu.VMEM((2, count, count), jnp.float32),
        in_specs=[pl.BlockSpec(memory_space=pl.ANY)],
        out_specs=pl.BlockSpec(memory_space=pltpu.VMEM),
        compiler_params=pltpu.CompilerParams(vmem_limit_bytes=8 << 20),
        name="green",
    )(message)
    message = exchange(message)
    cosine, sine = dft_tables(count)
    tables = split_table(np.concatenate([cosine, sine]))
    message = vmem_call(plane_kernel, exchanged, 24 << 20, (green, message, *tables))
    message = exchange(message)

    weight = np.full((half, 1), 2.0)
    weight[0] = 1.0
    tables = split_table(np.concatenate([forward_real * weight, forward_imag * weight]))
    potential = vmem_call(inverse_kernel, block, 12 << 20, (message, *tables))
    return density, potential


def ring(dx, dz):
    pairs = []
    for z in range(2):
        for x in range(4):
            for slab in range(16):
                target = (z + dz) % 2 * 4 + (x + dx) % 4
                pairs.append(((z * 4 + x) * 16 + slab, target * 16 + slab))
    return pairs


def band_sum(orbitals, occupation):
    def send(values, dx, dz):
        return lax.ppermute(values, axes, ring(dx, dz))

    far0, far1, cross2 = partial_densities(
        orbitals, occupation, [[(0, 2, 0)], [(0, 2, 1)], [(1, 2, 1)]]
    )
    far0 = send(far0, 1, 0)
    far1 = send(far1, -1, 0)
    cross2 = send(cross2, 0, 1)
    cross1, right1, left0, cross3 = partial_densities(
        orbitals, occupation, [[(1, 1, 1)], [(0, 1, 1)], [(0, 3, 0)], [(1, 3, 1)]]
    )
    cross1 = send(cross1, 0, 1)
    from_left1 = send(right1, 1, 0)
    from_right0 = send(left0, -1, 0)
    left1, right0, line2, cross4, line1, line3, own1, own0, line0 = partial_densities(
        orbitals,
        occupation,
        [
            [(0, 3, 1)],
            [(0, 1, 0)],
            [(1, 2, 0)],
            [(1, 0, 1)],
            [(1, 1, 0)],
            [(1, 3, 0)],
            [(0, 0, 1)],
            [(0, 0, 0)],
            [(1, 0, 0)],
        ],
    )
    from_left0 = send(right0 + far0, 1, 0)
    from_right1 = send(left1 + far1, -1, 0)
    cross3 = send(cross3, 0, 1)
    cross4 = send(cross4, 0, 1)
    half = planes[1] // 2 + 1
    line2 = line2 + cross2
    ahead = send(line2[:half], 1, 0)
    behind = send(line2[half:], -1, 0)
    line1 = line1 + cross1
    line1 = lax.dynamic_update_slice(line1, line1[:half] + ahead, (0, 0, 0))
    lines1 = send(line1, 1, 0)
    line3 = line3 + cross3
    line3 = lax.dynamic_update_slice(line3, line3[half:] + behind, (half, 0, 0))
    lines3 = send(line3, -1, 0)
    other = send(own1 + from_left1 + from_right1, 0, 1)
    upper = ((own0 + from_left0) + from_right0) + other
    lower = (line0 + cross4) + (lines1 + lines3)
    return upper, lower


def solution(mesh):
    in_specs = (P("band", "slab", None, None), P("band"))
    out_specs = (P("slab", "band", None), P("slab", "band", None))
    return jax.shard_map(solve, mesh=mesh, in_specs=in_specs, out_specs=out_specs, check_vma=False)
```

```python
import math

import jax
import jax.numpy as jnp
import numpy as np
from jax import lax
from jax.experimental import pallas as pl
from jax.experimental.pallas import tpu as pltpu
from jax.sharding import PartitionSpec as P


spacing = 0.08
axes = ("band", "slab")
planes = (9, 7)
cut = planes[1] // 2 + 1
piece_bytes = 576 << 10
spare_bytes = 4 << 20


def circle_tables(count):
    quarter = count // 4
    eighth = np.sin(2.0 * np.pi * np.arange(quarter + 1) / count)
    eighth[quarter] = 1.0
    first = np.concatenate([eighth[:quarter], eighth[:0:-1]])
    sine = np.concatenate([first, -first])
    cosine = np.roll(sine, -quarter)
    return cosine, sine


def split_table(table):
    high = table.astype(jnp.bfloat16)
    low = (table - high.astype(np.float64)).astype(jnp.bfloat16)
    return high, low


def dft_tables(count):
    cosine, sine = circle_tables(count)
    phases = np.arange(count)[:, None] * np.arange(count)[None, :] % count
    return cosine[phases], sine[phases]


def line_tables(count):
    cosine, sine = dft_tables(count)
    half = count // 2
    real_rows = cosine[:half].copy()
    imag_rows = -sine[:half]
    imag_rows[0] = cosine[half]
    return real_rows, imag_rows


def split(values):
    high = values.astype(jnp.bfloat16)
    low = (values - high.astype(jnp.float32)).astype(jnp.bfloat16)
    return high, low


def dot3(left, right, dims):
    first = jnp.concatenate([left[0], left[1], left[0]], axis=dims[0][0])
    second = jnp.concatenate([right[0], right[0], right[1]], axis=dims[1][0])
    return lax.dot_general(
        first, second, (dims, ((), ())), preferred_element_type=jnp.float32
    )


plain = ((1,), (0,))
rows_rows = ((1,), (1,))


def swap_blocks(parts):
    lane = lax.broadcasted_iota(jnp.int32, parts[0].shape, len(parts[0].shape) - 1)
    axis = len(parts[0].shape) - 1
    even = (lane // 32) % 2 == 0
    low = lane < 64
    pairs = []
    for first, second in ((parts[0], parts[1]), (parts[2], parts[3])):
        pairs.append(
            (
                jnp.where(even, first, pltpu.roll(second, 32, axis)),
                jnp.where(even, pltpu.roll(first, 96, axis), second),
            )
        )
    results = []
    for first, second in zip(*pairs):
        turned = pltpu.roll(jnp.where(low, second, first), 64, axis)
        results.append((jnp.where(low, first, turned), jnp.where(low, turned, second)))
    return [pair[0] for pair in results] + [pair[1] for pair in results]


def forward_kernel(
    own_ref, left_ref, right_ref, other_ref, line_ref, cross_ref, lines3_ref, lines1_ref, ahead_ref,
    high_ref, low_ref, density_ref, out_ref,
):
    depth = planes[0]
    density_ref[:depth] = (own_ref[...] + left_ref[...]) + (right_ref[...] + other_ref[...])
    lower = (line_ref[...] + cross_ref[1]) + lines3_ref[...]
    density_ref[depth : depth + cut] = lower[:cut] + lines1_ref[...]
    density_ref[depth + cut :] = lower[cut:] + ahead_ref[cut:]
    planes_of = [density_ref[z] for z in range(16)]
    rows = jnp.concatenate([planes_of[zh * 8 + zq] for zq in range(8) for zh in range(2)], axis=0)
    mean = jnp.sum(rows) * (1.0 / rows.size)
    lines = dot3((high_ref[...], low_ref[...]), split(rows - mean), rows_rows)
    zero = lax.broadcasted_iota(jnp.int32, (128, 512), 0) == 0
    real = lines[:128] + jnp.where(zero, mean * rows.shape[1], 0.0)
    imag = lines[128:]
    low = lax.broadcasted_iota(jnp.int32, (128, 128), 1) < 64
    for pair in range(4):
        a = real[:, pair * 128 : (pair + 1) * 128]
        b = imag[:, pair * 128 : (pair + 1) * 128]
        out_ref[pl.ds(2 * pair, 128, stride=8), :] = jnp.where(low, a, pltpu.roll(b, 64, 1))
        out_ref[pl.ds(2 * pair + 1, 128, stride=8), :] = jnp.where(low, pltpu.roll(a, 64, 1), b)


def plane_kernel(green_ref, message_ref, high_ref, low_ref, out_ref):
    count = 256
    stacked = (high_ref[...], low_ref[...])
    beside = [jnp.concatenate([table[:count], table[count:]], axis=1) for table in stacked]
    tile = jnp.sum(message_ref[...].reshape(128, 8, 128), axis=0)
    real_lane = lax.broadcasted_iota(jnp.int32, tile.shape, 1) < 64
    means = [
        jnp.sum(jnp.where(real_lane == keep, tile, 0.0)) * (1.0 / count**2) for keep in (True, False)
    ]
    reals, imags = [], []
    chunks = 1
    slabs = 16 // chunks
    rows = count // chunks
    for chunk in range(chunks):
        columns = [[], []]
        for group in range(2):
            parts = [
                message_ref[pl.ds((member * 16 + chunk * slabs) * 8, slabs * 8), :].reshape(
                    slabs, 8, 128
                )
                for member in range(group * 4, group * 4 + 4)
            ]
            blocks = swap_blocks(parts)
            for part in range(2):
                whole = jnp.stack([blocks[part * 2], blocks[part * 2 + 1]], axis=1)
                columns[part].append(whole.reshape(rows, 128))
        halves = [jnp.concatenate(columns[part], axis=1) - means[part] for part in range(2)]
        both = dot3(split(jnp.concatenate(halves, axis=0)), beside, plain)
        by_cos, by_sin = both[:, :count], both[:, count:]
        reals.append(by_cos[:rows] + by_sin[rows:])
        imags.append(by_cos[rows:] - by_sin[:rows])
    real = jnp.concatenate(reals, axis=0)
    imag = jnp.concatenate(imags, axis=0)
    both = dot3(stacked, split(jnp.concatenate([real, imag], axis=1)), plain)
    by_cos, by_sin = both[:count], both[count:]
    real = by_cos[:, :count] + by_sin[:, count:]
    imag = by_cos[:, count:] - by_sin[:, :count]
    zero = (lax.broadcasted_iota(jnp.int32, (count, count), 0) == 0) & (
        lax.broadcasted_iota(jnp.int32, (count, count), 1) == 0
    )
    real = real + jnp.where(zero, means[0] * count**2, 0.0)
    imag = imag + jnp.where(zero, means[1] * count**2, 0.0)
    green_a = green_ref[0]
    green_b = green_ref[1]
    operand = split(
        jnp.concatenate([real * green_a, imag * green_a, real * green_b, imag * green_b], axis=1)
    )
    both = dot3(stacked, operand, plain)
    by_cos, by_sin = both[:count], both[count:]
    real_a = by_cos[:, :count] - by_sin[:, count : 2 * count]
    imag_a = by_cos[:, count : 2 * count] + by_sin[:, :count]
    real_b = by_cos[:, 2 * count : 3 * count] - by_sin[:, 3 * count :]
    imag_b = by_cos[:, 3 * count :] + by_sin[:, 2 * count : 3 * count]
    for chunk in range(chunks):
        piece = slice(chunk * rows, (chunk + 1) * rows)
        pair = jnp.concatenate(
            [
                jnp.concatenate([real_a[piece], -imag_a[piece]], axis=1),
                jnp.concatenate([imag_b[piece], real_b[piece]], axis=1),
            ],
            axis=0,
        )
        result = dot3(split(pair), stacked, plain)
        for group in range(2):
            blocks = []
            for part in range(2):
                whole = result[part * rows : (part + 1) * rows, group * 128 : (group + 1) * 128]
                whole = whole.reshape(slabs, 2, 8, 128)
                blocks += [whole[:, 0], whole[:, 1]]
            for member, values in enumerate(swap_blocks(blocks), group * 4):
                place = pl.ds((member * 16 + chunk * slabs) * 8, slabs * 8)
                out_ref[place, :] = values.reshape(slabs * 8, 128)


def green_kernel(after_ref, out_ref):
    del after_ref
    count = 256
    rank = lax.axis_index("band") * lax.axis_size("slab") + lax.axis_index("slab")

    def signed(axis):
        index = lax.broadcasted_iota(jnp.int32, (count, count), axis)
        return jnp.where(index < count // 2, index, index - count).astype(jnp.float32)

    freq_z, freq_x = signed(0), signed(1)
    scale = (2.0 * math.pi / (count * spacing)) ** 2
    for place, freq in enumerate((rank, jnp.where(rank == 0, count // 2, rank))):
        freq_y = freq.astype(jnp.float32)
        wave_sq = scale * (freq_z * freq_z + freq_x * freq_x + freq_y * freq_y)
        anchor = wave_sq == 0.0
        out_ref[place] = jnp.where(
            anchor, 0.0, (4.0 * math.pi / count**3) / (wave_sq + anchor.astype(jnp.float32))
        )


def inverse_kernel(message_ref, high_ref, low_ref, out_ref):
    turned = [message_ref[pl.ds(zq, 128, stride=8), :].T for zq in range(8)]
    rows = jnp.concatenate(
        [jnp.concatenate([block[:64] for block in turned], axis=0),
         jnp.concatenate([block[64:] for block in turned], axis=0)], axis=1
    )
    lines = dot3(split(rows), (high_ref[...], low_ref[...]), plain)
    for zq in range(8):
        out_ref[zq] = lines[zq * 64 : zq * 64 + 32]
        out_ref[zq + 8] = lines[zq * 64 + 32 : zq * 64 + 64]


def density_kernel(pieces, occupation_ref, orbitals_ref, *refs):
    outs, (buffer, weights_ref, sems) = refs[:-3], refs[-3:]
    flat = [piece for group in pieces for piece in group]
    copies = []
    rank = lax.axis_index("band")
    for slot, (half, dx, dz) in enumerate(flat):
        block = (rank + 4 * dz) // 4 % 2 * 4 + (rank + dx) % 4
        depth = planes[half]
        source = orbitals_ref.at[:, pl.ds(half * planes[0], depth), pl.ds(block * 32, 32), :]
        target = buffer.at[slot, :, pl.ds(0, depth)]
        copies.append(pltpu.make_async_copy(source, target, sems.at[slot]))
    weigh = pltpu.make_async_copy(occupation_ref, weights_ref, sems.at[len(flat)])
    for copy in [weigh, *copies]:
        copy.start()
    weigh.wait()
    weights = [weights_ref[band] for band in range(4)]
    slot = 0
    for out, group in zip(outs, pieces):
        for place in range(len(group)):
            copies[slot].wait()
            total = None
            for band in range(4):
                values = buffer[slot, band, : planes[group[place][0]]].astype(jnp.float32)
                term = values * values * weights[band]
                total = term if total is None else total + term
            if len(group) == 1:
                out[...] = total
            else:
                out[place] = total
            slot += 1


def lines_kernel(cross_ref, line2_ref, line1_ref, ahead_out, behind_out):
    line = line2_ref[...] + cross_ref[0]
    ahead_out[:cut] = line[:cut]
    ahead_out[cut:] = line1_ref[cut:] + cross_ref[1, cut:]
    behind_out[...] = line[cut:]


def last_kernel(line_ref, cross_ref, behind_ref, out_ref):
    line = line_ref[...] + cross_ref[0]
    out_ref[:cut] = line[:cut]
    out_ref[cut:] = line[cut:] + behind_ref[...]


def partial_densities(orbitals, occupation, pieces):
    shapes = [
        pltpu.VMEM((len(g),) * (len(g) > 1) + (planes[g[0][0]], 32, 256), jnp.float32)
        for g in pieces
    ]
    count = sum(len(g) for g in pieces)
    limit = count * piece_bytes * 2 + spare_bytes
    return pl.pallas_call(
        lambda *refs: density_kernel(pieces, *refs),
        out_shape=shapes,
        in_specs=[pl.BlockSpec(memory_space=pltpu.HBM)] * 2,
        out_specs=[pl.BlockSpec(memory_space=pltpu.VMEM)] * len(shapes),
        scratch_shapes=[
            pltpu.VMEM((count, 4, max(planes), 32, 256), jnp.bfloat16),
            pltpu.SMEM((4,), jnp.float32),
            pltpu.SemaphoreType.DMA((count + 1,)),
        ],
        compiler_params=pltpu.CompilerParams(vmem_limit_bytes=limit),
    )(*[pltpu.with_memory_space_constraint(value, pltpu.HBM) for value in (occupation, orbitals)])


def vmem_call(kernel, out_shape, limit, operands):
    placed = [pltpu.with_memory_space_constraint(value, pltpu.VMEM) for value in operands]
    vmem = pl.BlockSpec(memory_space=pltpu.VMEM)
    return pl.pallas_call(
        kernel,
        out_shape=out_shape,
        in_specs=[vmem] * len(placed),
        out_specs=jax.tree.map(lambda shape: vmem, out_shape),
        compiler_params=pltpu.CompilerParams(vmem_limit_bytes=limit),
    )(*placed)


def exchange(message):
    return lax.all_to_all(message, axes, 0, 0, tiled=True)


def solve(orbitals, occupation):
    count = orbitals.shape[2]
    half = count // 2
    terms = band_sum(orbitals, occupation)

    forward_real, forward_imag = line_tables(count)
    tables = split_table(np.concatenate([forward_real, forward_imag]))
    block = jax.ShapeDtypeStruct((16, 32, count), jnp.float32)
    exchanged = pltpu.VMEM((half * 8, 128), jnp.float32)
    density = pltpu.VMEM((16, 32, count), jnp.float32)
    density, message = vmem_call(forward_kernel, [density, exchanged], 12 << 20, (*terms, *tables))
    green = pl.pallas_call(
        green_kernel,
        out_shape=pltpu.VMEM((2, count, count), jnp.float32),
        in_specs=[pl.BlockSpec(memory_space=pl.ANY)],
        out_specs=pl.BlockSpec(memory_space=pltpu.VMEM),
        compiler_params=pltpu.CompilerParams(vmem_limit_bytes=8 << 20),
        name="green",
    )(message)
    message = exchange(message)
    cosine, sine = dft_tables(count)
    tables = split_table(np.concatenate([cosine, sine]))
    message = vmem_call(plane_kernel, exchanged, 24 << 20, (green, message, *tables))
    message = exchange(message)

    weight = np.full((half, 1), 2.0)
    weight[0] = 1.0
    tables = split_table(np.concatenate([forward_real * weight, forward_imag * weight]))
    potential = vmem_call(inverse_kernel, block, 12 << 20, (message, *tables))
    return density, potential


def ring(dx, dz):
    pairs = []
    for z in range(2):
        for x in range(4):
            for slab in range(16):
                target = (z + dz) % 2 * 4 + (x + dx) % 4
                pairs.append(((z * 4 + x) * 16 + slab, target * 16 + slab))
    return pairs


def band_sum(orbitals, occupation):
    def send(values, dx, dz):
        return lax.ppermute(values, axes, ring(dx, dz))

    far0, far1, cross0 = partial_densities(
        orbitals, occupation, [[(0, 2, 0)], [(0, 2, 1)], [(1, 2, 1), (1, 1, 1)]]
    )
    far0 = send(far0, 1, 0)
    far1 = send(far1, -1, 0)
    cross0 = send(cross0, 0, 1)
    right1, left0, cross1 = partial_densities(
        orbitals, occupation, [[(0, 1, 1)], [(0, 3, 0)], [(1, 3, 1), (1, 0, 1)]]
    )
    right1 = send(right1, 1, 0)
    left0 = send(left0, -1, 0)
    left1, right0, line2, line1, line3, own1, own0, line0 = partial_densities(
        orbitals,
        occupation,
        [
            [(0, 3, 1)],
            [(0, 1, 0)],
            [(1, 2, 0)],
            [(1, 1, 0)],
            [(1, 3, 0)],
            [(0, 0, 1)],
            [(0, 0, 0)],
            [(1, 0, 0)],
        ],
    )
    left1 = send(left1 + far1, -1, 0)
    right0 = send(right0 + far0, 1, 0)
    cross1 = send(cross1, 0, 1)
    ahead, behind = vmem_call(
        lines_kernel,
        [pltpu.VMEM((depth, 32, 256), jnp.float32) for depth in (planes[1], planes[1] - cut)],
        8 << 20,
        (cross0, line2, line1),
    )
    ahead = send(ahead, 1, 0)
    behind = send(behind, -1, 0)
    other = send(own1 + right1 + left1, 0, 1)
    lines1 = send(line1[:cut] + cross0[1, :cut] + ahead[:cut], 1, 0)
    to_left = vmem_call(
        last_kernel, pltpu.VMEM((planes[1], 32, 256), jnp.float32), 8 << 20, (line3, cross1, behind)
    )
    lines3 = send(to_left, -1, 0)
    return (own0, left0, right0, other, line0, cross1, lines3, lines1, ahead)


def solution(mesh):
    in_specs = (P("band", "slab", None, None), P("band"))
    out_specs = (P("slab", "band", None), P("slab", "band", None))
    return jax.shard_map(solve, mesh=mesh, in_specs=in_specs, out_specs=out_specs, check_vma=False)
```

```python
import math

import jax
import jax.numpy as jnp
import numpy as np
from jax import lax
from jax.experimental import pallas as pl
from jax.experimental.pallas import tpu as pltpu
from jax.sharding import PartitionSpec as P


spacing = 0.08
axes = ("band", "slab")
planes = (9, 7)
cut = planes[1] // 2 + 1
piece_bytes = 576 << 10
spare_bytes = 4 << 20


def circle_tables(count):
    quarter = count // 4
    eighth = np.sin(2.0 * np.pi * np.arange(quarter + 1) / count)
    eighth[quarter] = 1.0
    first = np.concatenate([eighth[:quarter], eighth[:0:-1]])
    sine = np.concatenate([first, -first])
    cosine = np.roll(sine, -quarter)
    return cosine, sine


def split_table(table):
    high = table.astype(jnp.bfloat16)
    low = (table - high.astype(np.float64)).astype(jnp.bfloat16)
    return high, low


def dft_tables(count):
    cosine, sine = circle_tables(count)
    phases = np.arange(count)[:, None] * np.arange(count)[None, :] % count
    return cosine[phases], sine[phases]


def line_tables(count):
    cosine, sine = dft_tables(count)
    half = count // 2
    real_rows = cosine[:half].copy()
    imag_rows = -sine[:half]
    imag_rows[0] = cosine[half]
    return real_rows, imag_rows


def split(values):
    high = values.astype(jnp.bfloat16)
    low = (values - high.astype(jnp.float32)).astype(jnp.bfloat16)
    return high, low


def dot3(left, right, dims):
    first = jnp.concatenate([left[0], left[1], left[0]], axis=dims[0][0])
    second = jnp.concatenate([right[0], right[0], right[1]], axis=dims[1][0])
    return lax.dot_general(
        first, second, (dims, ((), ())), preferred_element_type=jnp.float32
    )


plain = ((1,), (0,))
rows_rows = ((1,), (1,))


def swap_blocks(parts):
    lane = lax.broadcasted_iota(jnp.int32, parts[0].shape, len(parts[0].shape) - 1)
    axis = len(parts[0].shape) - 1
    even = (lane // 32) % 2 == 0
    low = lane < 64
    pairs = []
    for first, second in ((parts[0], parts[1]), (parts[2], parts[3])):
        pairs.append(
            (
                jnp.where(even, first, pltpu.roll(second, 32, axis)),
                jnp.where(even, pltpu.roll(first, 96, axis), second),
            )
        )
    results = []
    for first, second in zip(*pairs):
        turned = pltpu.roll(jnp.where(low, second, first), 64, axis)
        results.append((jnp.where(low, first, turned), jnp.where(low, turned, second)))
    return [pair[0] for pair in results] + [pair[1] for pair in results]


def forward_kernel(
    own_ref, left_ref, right_ref, other_ref, line_ref, cross_ref, lines3_ref, lines1_ref, ahead_ref,
    high_ref, low_ref, density_ref, out_ref,
):
    depth = planes[0]
    density_ref[:depth] = (own_ref[...] + left_ref[...]) + (right_ref[...] + other_ref[...])
    lower = (line_ref[...] + cross_ref[1]) + lines3_ref[...]
    density_ref[depth : depth + cut] = lower[:cut] + lines1_ref[...]
    density_ref[depth + cut :] = lower[cut:] + ahead_ref[cut:]
    planes_of = [density_ref[z] for z in range(16)]
    rows = jnp.concatenate([planes_of[zh * 8 + zq] for zq in range(8) for zh in range(2)], axis=0)
    some = rows[:128]
    mean = jnp.sum(some) * (1.0 / some.size)
    lines = dot3((high_ref[...], low_ref[...]), split(rows - mean), rows_rows)
    zero = lax.broadcasted_iota(jnp.int32, (128, 512), 0) == 0
    real = lines[:128] + jnp.where(zero, mean * rows.shape[1], 0.0)
    imag = lines[128:]
    low = lax.broadcasted_iota(jnp.int32, (128, 128), 1) < 64
    for pair in range(4):
        a = real[:, pair * 128 : (pair + 1) * 128]
        b = imag[:, pair * 128 : (pair + 1) * 128]
        turned = pltpu.roll(jnp.where(low, b, a), 64, 1)
        out_ref[pl.ds(2 * pair, 128, stride=8), :] = jnp.where(low, a, turned)
        out_ref[pl.ds(2 * pair + 1, 128, stride=8), :] = jnp.where(low, turned, b)


def plane_kernel(green_ref, message_ref, high_ref, low_ref, out_ref):
    count = 256
    stacked = (high_ref[...], low_ref[...])
    beside = [jnp.concatenate([table[:count], table[count:]], axis=1) for table in stacked]
    tile = jnp.sum(message_ref[...].reshape(128, 8, 128), axis=0)
    real_lane = lax.broadcasted_iota(jnp.int32, tile.shape, 1) < 64
    means = [
        jnp.sum(jnp.where(real_lane == keep, tile, 0.0)) * (1.0 / count**2) for keep in (True, False)
    ]
    reals, imags = [], []
    chunks = 1
    slabs = 16 // chunks
    rows = count // chunks
    for chunk in range(chunks):
        columns = [[], []]
        for group in range(2):
            parts = [
                message_ref[pl.ds((member * 16 + chunk * slabs) * 8, slabs * 8), :].reshape(
                    slabs, 8, 128
                )
                for member in range(group * 4, group * 4 + 4)
            ]
            blocks = swap_blocks(parts)
            for part in range(2):
                whole = jnp.stack([blocks[part * 2], blocks[part * 2 + 1]], axis=1)
                columns[part].append(whole.reshape(rows, 128))
        halves = [jnp.concatenate(columns[part], axis=1) - means[part] for part in range(2)]
        both = dot3(split(jnp.concatenate(halves, axis=0)), beside, plain)
        by_cos, by_sin = both[:, :count], both[:, count:]
        reals.append(by_cos[:rows] + by_sin[rows:])
        imags.append(by_cos[rows:] - by_sin[:rows])
    real = jnp.concatenate(reals, axis=0)
    imag = jnp.concatenate(imags, axis=0)
    both = dot3(stacked, split(jnp.concatenate([real, imag], axis=1)), plain)
    by_cos, by_sin = both[:count], both[count:]
    real = by_cos[:, :count] + by_sin[:, count:]
    imag = by_cos[:, count:] - by_sin[:, :count]
    zero = (lax.broadcasted_iota(jnp.int32, (count, count), 0) == 0) & (
        lax.broadcasted_iota(jnp.int32, (count, count), 1) == 0
    )
    real = real + jnp.where(zero, means[0] * count**2, 0.0)
    imag = imag + jnp.where(zero, means[1] * count**2, 0.0)
    green_a = green_ref[0]
    green_b = green_ref[1]
    operand = split(
        jnp.concatenate([real * green_a, imag * green_a, real * green_b, imag * green_b], axis=1)
    )
    both = dot3(stacked, operand, plain)
    by_cos, by_sin = both[:count], both[count:]
    real_a = by_cos[:, :count] - by_sin[:, count : 2 * count]
    imag_a = by_cos[:, count : 2 * count] + by_sin[:, :count]
    real_b = by_cos[:, 2 * count : 3 * count] - by_sin[:, 3 * count :]
    imag_b = by_cos[:, 3 * count :] + by_sin[:, 2 * count : 3 * count]
    for chunk in range(chunks):
        piece = slice(chunk * rows, (chunk + 1) * rows)
        pair = jnp.concatenate(
            [
                jnp.concatenate([real_a[piece], -imag_a[piece]], axis=1),
                jnp.concatenate([imag_b[piece], real_b[piece]], axis=1),
            ],
            axis=0,
        )
        result = dot3(split(pair), stacked, plain)
        for group in range(2):
            blocks = []
            for part in range(2):
                whole = result[part * rows : (part + 1) * rows, group * 128 : (group + 1) * 128]
                whole = whole.reshape(slabs, 2, 8, 128)
                blocks += [whole[:, 0], whole[:, 1]]
            for member, values in enumerate(swap_blocks(blocks), group * 4):
                place = pl.ds((member * 16 + chunk * slabs) * 8, slabs * 8)
                out_ref[place, :] = values.reshape(slabs * 8, 128)


def green_kernel(after_ref, out_ref):
    del after_ref
    count = 256
    rank = lax.axis_index("band") * lax.axis_size("slab") + lax.axis_index("slab")

    def signed(axis):
        index = lax.broadcasted_iota(jnp.int32, (count, count), axis)
        return jnp.where(index < count // 2, index, index - count).astype(jnp.float32)

    freq_z, freq_x = signed(0), signed(1)
    scale = (2.0 * math.pi / (count * spacing)) ** 2
    for place, freq in enumerate((rank, jnp.where(rank == 0, count // 2, rank))):
        freq_y = freq.astype(jnp.float32)
        wave_sq = scale * (freq_z * freq_z + freq_x * freq_x + freq_y * freq_y)
        anchor = wave_sq == 0.0
        out_ref[place] = jnp.where(
            anchor, 0.0, (4.0 * math.pi / count**3) / (wave_sq + anchor.astype(jnp.float32))
        )


def inverse_kernel(message_ref, high_ref, low_ref, out_ref):
    turned = [message_ref[pl.ds(zq, 128, stride=8), :].T for zq in range(8)]
    rows = jnp.concatenate(
        [jnp.concatenate([block[:64] for block in turned], axis=0),
         jnp.concatenate([block[64:] for block in turned], axis=0)], axis=1
    )
    lines = dot3(split(rows), (high_ref[...], low_ref[...]), plain)
    for zq in range(8):
        out_ref[zq] = lines[zq * 64 : zq * 64 + 32]
        out_ref[zq + 8] = lines[zq * 64 + 32 : zq * 64 + 64]


def density_kernel(pieces, occupation_ref, orbitals_ref, *refs):
    outs, (buffer, weights_ref, sems) = refs[:-3], refs[-3:]
    flat = [piece for group in pieces for piece in group]
    copies = []
    rank = lax.axis_index("band")
    for slot, (half, dx, dz) in enumerate(flat):
        block = (rank + 4 * dz) // 4 % 2 * 4 + (rank + dx) % 4
        depth = planes[half]
        source = orbitals_ref.at[:, pl.ds(half * planes[0], depth), pl.ds(block * 32, 32), :]
        target = buffer.at[slot, :, pl.ds(0, depth)]
        copies.append(pltpu.make_async_copy(source, target, sems.at[slot]))
    weigh = pltpu.make_async_copy(occupation_ref, weights_ref, sems.at[len(flat)])
    for copy in [weigh, *copies]:
        copy.start()
    weigh.wait()
    weights = [weights_ref[band] for band in range(4)]
    slot = 0
    for out, group in zip(outs, pieces):
        for place in range(len(group)):
            copies[slot].wait()
            total = None
            for band in range(4):
                values = buffer[slot, band, : planes[group[place][0]]].astype(jnp.float32)
                term = values * values * weights[band]
                total = term if total is None else total + term
            if len(group) == 1:
                out[...] = total
            else:
                out[place] = total
            slot += 1


def lines_kernel(cross_ref, line2_ref, line1_ref, ahead_out, behind_out):
    line = line2_ref[...] + cross_ref[0]
    ahead_out[:cut] = line[:cut]
    ahead_out[cut:] = line1_ref[cut:] + cross_ref[1, cut:]
    behind_out[...] = line[cut:]


def last_kernel(line_ref, cross_ref, behind_ref, out_ref):
    line = line_ref[...] + cross_ref[0]
    out_ref[:cut] = line[:cut]
    out_ref[cut:] = line[cut:] + behind_ref[...]


def partial_densities(orbitals, occupation, pieces):
    shapes = [
        pltpu.VMEM((len(g),) * (len(g) > 1) + (planes[g[0][0]], 32, 256), jnp.float32)
        for g in pieces
    ]
    count = sum(len(g) for g in pieces)
    limit = count * piece_bytes * 2 + spare_bytes
    return pl.pallas_call(
        lambda *refs: density_kernel(pieces, *refs),
        out_shape=shapes,
        in_specs=[pl.BlockSpec(memory_space=pltpu.HBM)] * 2,
        out_specs=[pl.BlockSpec(memory_space=pltpu.VMEM)] * len(shapes),
        scratch_shapes=[
            pltpu.VMEM((count, 4, max(planes), 32, 256), jnp.bfloat16),
            pltpu.SMEM((4,), jnp.float32),
            pltpu.SemaphoreType.DMA((count + 1,)),
        ],
        compiler_params=pltpu.CompilerParams(vmem_limit_bytes=limit),
    )(*[pltpu.with_memory_space_constraint(value, pltpu.HBM) for value in (occupation, orbitals)])


def vmem_call(kernel, out_shape, limit, operands):
    placed = [pltpu.with_memory_space_constraint(value, pltpu.VMEM) for value in operands]
    vmem = pl.BlockSpec(memory_space=pltpu.VMEM)
    return pl.pallas_call(
        kernel,
        out_shape=out_shape,
        in_specs=[vmem] * len(placed),
        out_specs=jax.tree.map(lambda shape: vmem, out_shape),
        compiler_params=pltpu.CompilerParams(vmem_limit_bytes=limit),
    )(*placed)


def exchange(message):
    return lax.all_to_all(message, axes, 0, 0, tiled=True)


def solve(orbitals, occupation):
    count = orbitals.shape[2]
    half = count // 2
    terms = band_sum(orbitals, occupation)

    forward_real, forward_imag = line_tables(count)
    tables = split_table(np.concatenate([forward_real, forward_imag]))
    block = jax.ShapeDtypeStruct((16, 32, count), jnp.float32)
    exchanged = pltpu.VMEM((half * 8, 128), jnp.float32)
    density = pltpu.VMEM((16, 32, count), jnp.float32)
    density, message = vmem_call(forward_kernel, [density, exchanged], 12 << 20, (*terms, *tables))
    green = pl.pallas_call(
        green_kernel,
        out_shape=pltpu.VMEM((2, count, count), jnp.float32),
        in_specs=[pl.BlockSpec(memory_space=pl.ANY)],
        out_specs=pl.BlockSpec(memory_space=pltpu.VMEM),
        compiler_params=pltpu.CompilerParams(vmem_limit_bytes=8 << 20),
        name="green",
    )(message)
    message = exchange(message)
    cosine, sine = dft_tables(count)
    tables = split_table(np.concatenate([cosine, sine]))
    message = vmem_call(plane_kernel, exchanged, 24 << 20, (green, message, *tables))
    message = exchange(message)

    weight = np.full((half, 1), 2.0)
    weight[0] = 1.0
    tables = split_table(np.concatenate([forward_real * weight, forward_imag * weight]))
    potential = vmem_call(inverse_kernel, block, 12 << 20, (message, *tables))
    return density, potential


def ring(dx, dz):
    pairs = []
    for z in range(2):
        for x in range(4):
            for slab in range(16):
                target = (z + dz) % 2 * 4 + (x + dx) % 4
                pairs.append(((z * 4 + x) * 16 + slab, target * 16 + slab))
    return pairs


def band_sum(orbitals, occupation):
    def send(values, dx, dz):
        return lax.ppermute(values, axes, ring(dx, dz))

    far0, far1, cross0 = partial_densities(
        orbitals, occupation, [[(0, 2, 0)], [(0, 2, 1)], [(1, 2, 1), (1, 1, 1)]]
    )
    far0 = send(far0, 1, 0)
    far1 = send(far1, -1, 0)
    cross0 = send(cross0, 0, 1)
    right1, left0, cross1 = partial_densities(
        orbitals, occupation, [[(0, 1, 1)], [(0, 3, 0)], [(1, 3, 1), (1, 0, 1)]]
    )
    right1 = send(right1, 1, 0)
    left0 = send(left0, -1, 0)
    left1, right0, line2, line1, line3, own1, own0, line0 = partial_densities(
        orbitals,
        occupation,
        [
            [(0, 3, 1)],
            [(0, 1, 0)],
            [(1, 2, 0)],
            [(1, 1, 0)],
            [(1, 3, 0)],
            [(0, 0, 1)],
            [(0, 0, 0)],
            [(1, 0, 0)],
        ],
    )
    left1 = send(left1 + far1, -1, 0)
    right0 = send(right0 + far0, 1, 0)
    cross1 = send(cross1, 0, 1)
    ahead, behind = vmem_call(
        lines_kernel,
        [pltpu.VMEM((depth, 32, 256), jnp.float32) for depth in (planes[1], planes[1] - cut)],
        8 << 20,
        (cross0, line2, line1),
    )
    ahead = send(ahead, 1, 0)
    behind = send(behind, -1, 0)
    other = send(own1 + right1 + left1, 0, 1)
    lines1 = send(line1[:cut] + cross0[1, :cut] + ahead[:cut], 1, 0)
    to_left = vmem_call(
        last_kernel, pltpu.VMEM((planes[1], 32, 256), jnp.float32), 8 << 20, (line3, cross1, behind)
    )
    lines3 = send(to_left, -1, 0)
    return (own0, left0, right0, other, line0, cross1, lines3, lines1, ahead)


def solution(mesh):
    in_specs = (P("band", "slab", None, None), P("band"))
    out_specs = (P("slab", "band", None), P("slab", "band", None))
    return jax.shard_map(solve, mesh=mesh, in_specs=in_specs, out_specs=out_specs, check_vma=False)
```

```python
import math

import jax
import jax.numpy as jnp
import numpy as np
from jax import lax
from jax.experimental import pallas as pl
from jax.experimental.pallas import tpu as pltpu
from jax.sharding import PartitionSpec as P


spacing = 0.08
axes = ("band", "slab")
planes = (9, 7)
cut = planes[1] // 2 + 1
piece_bytes = 576 << 10
spare_bytes = 4 << 20


def circle_tables(count):
    quarter = count // 4
    eighth = np.sin(2.0 * np.pi * np.arange(quarter + 1) / count)
    eighth[quarter] = 1.0
    first = np.concatenate([eighth[:quarter], eighth[:0:-1]])
    sine = np.concatenate([first, -first])
    cosine = np.roll(sine, -quarter)
    return cosine, sine


def split_table(table):
    high = table.astype(jnp.bfloat16)
    low = (table - high.astype(np.float64)).astype(jnp.bfloat16)
    return high, low


def dft_tables(count):
    cosine, sine = circle_tables(count)
    phases = np.arange(count)[:, None] * np.arange(count)[None, :] % count
    return cosine[phases], sine[phases]


def line_tables(count):
    cosine, sine = dft_tables(count)
    half = count // 2
    real_rows = cosine[:half].copy()
    imag_rows = -sine[:half]
    imag_rows[0] = cosine[half]
    return real_rows, imag_rows


def split(values):
    high = values.astype(jnp.bfloat16)
    low = (values - high.astype(jnp.float32)).astype(jnp.bfloat16)
    return high, low


def dot3(left, right, dims):
    first = jnp.concatenate([left[0], left[1], left[0]], axis=dims[0][0])
    second = jnp.concatenate([right[0], right[0], right[1]], axis=dims[1][0])
    return lax.dot_general(
        first, second, (dims, ((), ())), preferred_element_type=jnp.float32
    )


def dot3_apart(left, right, dims):
    def one(a, b):
        return lax.dot_general(a, b, (dims, ((), ())), preferred_element_type=jnp.float32)

    return one(left[0], right[0]) + (one(left[1], right[0]) + one(left[0], right[1]))


plain = ((1,), (0,))
rows_rows = ((1,), (1,))


def swap_blocks(parts):
    lane = lax.broadcasted_iota(jnp.int32, parts[0].shape, len(parts[0].shape) - 1)
    axis = len(parts[0].shape) - 1
    even = (lane // 32) % 2 == 0
    low = lane < 64
    pairs = []
    for first, second in ((parts[0], parts[1]), (parts[2], parts[3])):
        pairs.append(
            (
                jnp.where(even, first, pltpu.roll(second, 32, axis)),
                jnp.where(even, pltpu.roll(first, 96, axis), second),
            )
        )
    results = []
    for first, second in zip(*pairs):
        turned = pltpu.roll(jnp.where(low, second, first), 64, axis)
        results.append((jnp.where(low, first, turned), jnp.where(low, turned, second)))
    return [pair[0] for pair in results] + [pair[1] for pair in results]


def forward_kernel(
    own_ref, left_ref, right_ref, other_ref, line_ref, cross_ref, lines3_ref, lines1_ref, ahead_ref,
    high_ref, low_ref, density_ref, out_ref,
):
    depth = planes[0]
    density_ref[:depth] = (own_ref[...] + left_ref[...]) + (right_ref[...] + other_ref[...])
    lower = (line_ref[...] + cross_ref[1]) + lines3_ref[...]
    density_ref[depth : depth + cut] = lower[:cut] + lines1_ref[...]
    density_ref[depth + cut :] = lower[cut:] + ahead_ref[cut:]
    planes_of = [density_ref[z] for z in range(16)]
    rows = jnp.concatenate([planes_of[zh * 8 + zq] for zq in range(8) for zh in range(2)], axis=0)
    some = rows[:128]
    mean = jnp.sum(some) * (1.0 / some.size)
    lines = dot3((high_ref[...], low_ref[...]), split(rows - mean), rows_rows)
    zero = lax.broadcasted_iota(jnp.int32, (128, 512), 0) == 0
    real = lines[:128] + jnp.where(zero, mean * rows.shape[1], 0.0)
    imag = lines[128:]
    low = lax.broadcasted_iota(jnp.int32, (128, 128), 1) < 64
    for pair in range(4):
        a = real[:, pair * 128 : (pair + 1) * 128]
        b = imag[:, pair * 128 : (pair + 1) * 128]
        turned = pltpu.roll(jnp.where(low, b, a), 64, 1)
        out_ref[pl.ds(2 * pair, 128, stride=8), :] = jnp.where(low, a, turned)
        out_ref[pl.ds(2 * pair + 1, 128, stride=8), :] = jnp.where(low, turned, b)


def plane_kernel(green_ref, message_ref, high_ref, low_ref, out_ref):
    count = 256
    stacked = (high_ref[...], low_ref[...])
    beside = [jnp.concatenate([table[:count], table[count:]], axis=1) for table in stacked]
    tile = jnp.sum(message_ref[...].reshape(128, 8, 128), axis=0)
    real_lane = lax.broadcasted_iota(jnp.int32, tile.shape, 1) < 64
    means = [
        jnp.sum(jnp.where(real_lane == keep, tile, 0.0)) * (1.0 / count**2) for keep in (True, False)
    ]
    reals, imags = [], []
    chunks = 1
    slabs = 16 // chunks
    rows = count // chunks
    for chunk in range(chunks):
        columns = [[], []]
        for group in range(2):
            parts = [
                message_ref[pl.ds((member * 16 + chunk * slabs) * 8, slabs * 8), :].reshape(
                    slabs, 8, 128
                )
                for member in range(group * 4, group * 4 + 4)
            ]
            blocks = swap_blocks(parts)
            for part in range(2):
                whole = jnp.stack([blocks[part * 2], blocks[part * 2 + 1]], axis=1)
                columns[part].append(whole.reshape(rows, 128))
        halves = [jnp.concatenate(columns[part], axis=1) - means[part] for part in range(2)]
        both = dot3(split(jnp.concatenate(halves, axis=0)), beside, plain)
        by_cos, by_sin = both[:, :count], both[:, count:]
        reals.append(by_cos[:rows] + by_sin[rows:])
        imags.append(by_cos[rows:] - by_sin[:rows])
    real = jnp.concatenate(reals, axis=0)
    imag = jnp.concatenate(imags, axis=0)
    both = dot3(stacked, split(jnp.concatenate([real, imag], axis=1)), plain)
    by_cos, by_sin = both[:count], both[count:]
    real = by_cos[:, :count] + by_sin[:, count:]
    imag = by_cos[:, count:] - by_sin[:, :count]
    zero = (lax.broadcasted_iota(jnp.int32, (count, count), 0) == 0) & (
        lax.broadcasted_iota(jnp.int32, (count, count), 1) == 0
    )
    real = real + jnp.where(zero, means[0] * count**2, 0.0)
    imag = imag + jnp.where(zero, means[1] * count**2, 0.0)
    green_a = green_ref[0]
    green_b = green_ref[1]
    operand = split(
        jnp.concatenate([real * green_a, imag * green_a, real * green_b, imag * green_b], axis=1)
    )
    both = dot3_apart(stacked, operand, plain)
    by_cos, by_sin = both[:count], both[count:]
    real_a = by_cos[:, :count] - by_sin[:, count : 2 * count]
    imag_a = by_cos[:, count : 2 * count] + by_sin[:, :count]
    real_b = by_cos[:, 2 * count : 3 * count] - by_sin[:, 3 * count :]
    imag_b = by_cos[:, 3 * count :] + by_sin[:, 2 * count : 3 * count]
    for chunk in range(chunks):
        piece = slice(chunk * rows, (chunk + 1) * rows)
        pair = jnp.concatenate(
            [
                jnp.concatenate([real_a[piece], -imag_a[piece]], axis=1),
                jnp.concatenate([imag_b[piece], real_b[piece]], axis=1),
            ],
            axis=0,
        )
        result = dot3(split(pair), stacked, plain)
        for group in range(2):
            blocks = []
            for part in range(2):
                whole = result[part * rows : (part + 1) * rows, group * 128 : (group + 1) * 128]
                whole = whole.reshape(slabs, 2, 8, 128)
                blocks += [whole[:, 0], whole[:, 1]]
            for member, values in enumerate(swap_blocks(blocks), group * 4):
                place = pl.ds((member * 16 + chunk * slabs) * 8, slabs * 8)
                out_ref[place, :] = values.reshape(slabs * 8, 128)


def green_kernel(after_ref, out_ref):
    del after_ref
    count = 256
    rank = lax.axis_index("band") * lax.axis_size("slab") + lax.axis_index("slab")

    def signed(axis):
        index = lax.broadcasted_iota(jnp.int32, (count, count), axis)
        return jnp.where(index < count // 2, index, index - count).astype(jnp.float32)

    freq_z, freq_x = signed(0), signed(1)
    scale = (2.0 * math.pi / (count * spacing)) ** 2
    for place, freq in enumerate((rank, jnp.where(rank == 0, count // 2, rank))):
        freq_y = freq.astype(jnp.float32)
        wave_sq = scale * (freq_z * freq_z + freq_x * freq_x + freq_y * freq_y)
        anchor = wave_sq == 0.0
        out_ref[place] = jnp.where(
            anchor, 0.0, (4.0 * math.pi / count**3) / (wave_sq + anchor.astype(jnp.float32))
        )


def inverse_kernel(message_ref, high_ref, low_ref, out_ref):
    turned = [message_ref[pl.ds(zq, 128, stride=8), :].T for zq in range(8)]
    rows = jnp.concatenate(
        [jnp.concatenate([block[:64] for block in turned], axis=0),
         jnp.concatenate([block[64:] for block in turned], axis=0)], axis=1
    )
    lines = dot3(split(rows), (high_ref[...], low_ref[...]), plain)
    for zq in range(8):
        out_ref[zq] = lines[zq * 64 : zq * 64 + 32]
        out_ref[zq + 8] = lines[zq * 64 + 32 : zq * 64 + 64]


def density_kernel(pieces, occupation_ref, orbitals_ref, *refs):
    outs, (buffer, weights_ref, sems) = refs[:-3], refs[-3:]
    flat = [piece for group in pieces for piece in group]
    copies = []
    rank = lax.axis_index("band")
    for slot, (half, dx, dz) in enumerate(flat):
        block = (rank + 4 * dz) // 4 % 2 * 4 + (rank + dx) % 4
        depth = planes[half]
        source = orbitals_ref.at[:, pl.ds(half * planes[0], depth), pl.ds(block * 32, 32), :]
        target = buffer.at[slot, :, pl.ds(0, depth)]
        copies.append(pltpu.make_async_copy(source, target, sems.at[slot]))
    weigh = pltpu.make_async_copy(occupation_ref, weights_ref, sems.at[len(flat)])
    for copy in [weigh, *copies]:
        copy.start()
    weigh.wait()
    weights = [weights_ref[band] for band in range(4)]
    slot = 0
    for out, group in zip(outs, pieces):
        for place in range(len(group)):
            copies[slot].wait()
            total = None
            for band in range(4):
                values = buffer[slot, band, : planes[group[place][0]]].astype(jnp.float32)
                term = values * values * weights[band]
                total = term if total is None else total + term
            if len(group) == 1:
                out[...] = total
            else:
                out[place] = total
            slot += 1


def lines_kernel(cross_ref, line2_ref, line1_ref, ahead_out, behind_out):
    line = line2_ref[...] + cross_ref[0]
    ahead_out[:cut] = line[:cut]
    ahead_out[cut:] = line1_ref[cut:] + cross_ref[1, cut:]
    behind_out[...] = line[cut:]


def last_kernel(line_ref, cross_ref, behind_ref, out_ref):
    line = line_ref[...] + cross_ref[0]
    out_ref[:cut] = line[:cut]
    out_ref[cut:] = line[cut:] + behind_ref[...]


def partial_densities(orbitals, occupation, pieces):
    shapes = [
        pltpu.VMEM((len(g),) * (len(g) > 1) + (planes[g[0][0]], 32, 256), jnp.float32)
        for g in pieces
    ]
    count = sum(len(g) for g in pieces)
    limit = count * piece_bytes * 2 + spare_bytes
    return pl.pallas_call(
        lambda *refs: density_kernel(pieces, *refs),
        out_shape=shapes,
        in_specs=[pl.BlockSpec(memory_space=pltpu.HBM)] * 2,
        out_specs=[pl.BlockSpec(memory_space=pltpu.VMEM)] * len(shapes),
        scratch_shapes=[
            pltpu.VMEM((count, 4, max(planes), 32, 256), jnp.bfloat16),
            pltpu.SMEM((4,), jnp.float32),
            pltpu.SemaphoreType.DMA((count + 1,)),
        ],
        compiler_params=pltpu.CompilerParams(vmem_limit_bytes=limit),
    )(*[pltpu.with_memory_space_constraint(value, pltpu.HBM) for value in (occupation, orbitals)])


def vmem_call(kernel, out_shape, limit, operands):
    placed = [pltpu.with_memory_space_constraint(value, pltpu.VMEM) for value in operands]
    vmem = pl.BlockSpec(memory_space=pltpu.VMEM)
    return pl.pallas_call(
        kernel,
        out_shape=out_shape,
        in_specs=[vmem] * len(placed),
        out_specs=jax.tree.map(lambda shape: vmem, out_shape),
        compiler_params=pltpu.CompilerParams(vmem_limit_bytes=limit),
    )(*placed)


def exchange(message):
    return lax.all_to_all(message, axes, 0, 0, tiled=True)


def solve(orbitals, occupation):
    count = orbitals.shape[2]
    half = count // 2
    terms = band_sum(orbitals, occupation)

    forward_real, forward_imag = line_tables(count)
    tables = split_table(np.concatenate([forward_real, forward_imag]))
    block = jax.ShapeDtypeStruct((16, 32, count), jnp.float32)
    exchanged = pltpu.VMEM((half * 8, 128), jnp.float32)
    density = pltpu.VMEM((16, 32, count), jnp.float32)
    density, message = vmem_call(forward_kernel, [density, exchanged], 12 << 20, (*terms, *tables))
    green = pl.pallas_call(
        green_kernel,
        out_shape=pltpu.VMEM((2, count, count), jnp.float32),
        in_specs=[pl.BlockSpec(memory_space=pl.ANY)],
        out_specs=pl.BlockSpec(memory_space=pltpu.VMEM),
        compiler_params=pltpu.CompilerParams(vmem_limit_bytes=8 << 20),
        name="green",
    )(message)
    message = exchange(message)
    cosine, sine = dft_tables(count)
    tables = split_table(np.concatenate([cosine, sine]))
    message = vmem_call(plane_kernel, exchanged, 24 << 20, (green, message, *tables))
    message = exchange(message)

    weight = np.full((half, 1), 2.0)
    weight[0] = 1.0
    tables = split_table(np.concatenate([forward_real * weight, forward_imag * weight]))
    potential = vmem_call(inverse_kernel, block, 12 << 20, (message, *tables))
    return density, potential


def ring(dx, dz):
    pairs = []
    for z in range(2):
        for x in range(4):
            for slab in range(16):
                target = (z + dz) % 2 * 4 + (x + dx) % 4
                pairs.append(((z * 4 + x) * 16 + slab, target * 16 + slab))
    return pairs


def band_sum(orbitals, occupation):
    def send(values, dx, dz):
        return lax.ppermute(values, axes, ring(dx, dz))

    far0, far1, cross0 = partial_densities(
        orbitals, occupation, [[(0, 2, 0)], [(0, 2, 1)], [(1, 2, 1), (1, 1, 1)]]
    )
    far0 = send(far0, 1, 0)
    far1 = send(far1, -1, 0)
    cross0 = send(cross0, 0, 1)
    right1, left0, cross1 = partial_densities(
        orbitals, occupation, [[(0, 1, 1)], [(0, 3, 0)], [(1, 3, 1), (1, 0, 1)]]
    )
    right1 = send(right1, 1, 0)
    left0 = send(left0, -1, 0)
    left1, right0, line2, line1, line3, own1, own0, line0 = partial_densities(
        orbitals,
        occupation,
        [
            [(0, 3, 1)],
            [(0, 1, 0)],
            [(1, 2, 0)],
            [(1, 1, 0)],
            [(1, 3, 0)],
            [(0, 0, 1)],
            [(0, 0, 0)],
            [(1, 0, 0)],
        ],
    )
    left1 = send(left1 + far1, -1, 0)
    right0 = send(right0 + far0, 1, 0)
    cross1 = send(cross1, 0, 1)
    ahead, behind = vmem_call(
        lines_kernel,
        [pltpu.VMEM((depth, 32, 256), jnp.float32) for depth in (planes[1], planes[1] - cut)],
        8 << 20,
        (cross0, line2, line1),
    )
    ahead = send(ahead, 1, 0)
    behind = send(behind, -1, 0)
    other = send(own1 + right1 + left1, 0, 1)
    lines1 = send(line1[:cut] + cross0[1, :cut] + ahead[:cut], 1, 0)
    to_left = vmem_call(
        last_kernel, pltpu.VMEM((planes[1], 32, 256), jnp.float32), 8 << 20, (line3, cross1, behind)
    )
    lines3 = send(to_left, -1, 0)
    return (own0, left0, right0, other, line0, cross1, lines3, lines1, ahead)


def solution(mesh):
    in_specs = (P("band", "slab", None, None), P("band"))
    out_specs = (P("slab", "band", None), P("slab", "band", None))
    return jax.shard_map(solve, mesh=mesh, in_specs=in_specs, out_specs=out_specs, check_vma=False)
```
